128 devices in a mesh: seq: 8 (over z, core), exp: 16 (over y, x).
Axes of the slice: x: 4, y: 4, z: 4, core: 2. Of those that a mesh axis runs over, the one named last changes fastest.
Arguments:
- tokens: bfloat16 [32768, 4096], P(('seq', 'exp')), may hold values from -3 to 3
- cotangent: bfloat16 [32768, 4096], P(('seq', 'exp')), may hold values from -2 to 2
- router: bfloat16 [4096, 16], replicated, may hold values from -0.09375 to 0.09375
- threshold: float32 [16], replicated, may hold values from -1 to 1
- w_gate: bfloat16 [16, 4096, 1536], P('exp', None, 'seq'), may hold values from -0.09375 to 0.09375
- w_up: bfloat16 [16, 4096, 1536], P('exp', None, 'seq'), may hold values from -0.09375 to 0.09375
- w_down: bfloat16 [16, 1536, 4096], P('exp', 'seq'), may hold values from -0.15625 to 0.15625
- hid_scale: float32 [16, 1536], P('exp', 'seq'), may hold values from 0.5 to 2
- picks: int32 [128, 16, 4], P(('seq', 'exp')), may hold values from 0 to 255, as said below
- counts: int32 [128, 16], P(('seq', 'exp')), may hold values from 1 to 4, as said below
Outputs:
- mixture: bfloat16 [32768, 4096], P(('seq', 'exp'))
- token_grad: bfloat16 [32768, 4096], P(('seq', 'exp'))
- router_grad: float32 [4096, 16], P(('seq', 'exp'))
- threshold_grad: float32 [16], replicated
- gate_grad: float32 [16, 4096, 1536], P('exp', None, 'seq')
- up_grad: float32 [16, 4096, 1536], P('exp', None, 'seq')
- down_grad: float32 [16, 1536, 4096], P('exp', 'seq')
The draws below stay inside these ranges and needn't reach their ends.
Inputs may be any that keep to these rules, and one draw needn't show every extreme that they name: Each list picks[p, e] holds 4 distinct local rows of owner p. `counts`: for every expert some owner fills all 4 slots.
All inputs are finite; a program needn't handle non-finite values.
Results may differ from the reference program's by a relative error of at most 0.018.
Values may be sent and summed in bfloat16 or wider, within the bound.
A program may use at most 128 MiB of HBM per device.

```python
import math
import jax
import jax.numpy as jnp
from jax import lax

D = 4096
HID = 1536
TOK_DEV = 256
SLOT = 4
EXPERTS = 16
OWNERS = 128
TOKENS = 32768
N_SEQ = 8


def draw_picks(key, part):
    noise = jax.random.randint(jax.random.fold_in(key, 11), (OWNERS, EXPERTS, TOK_DEV), 0, 2 ** 20)
    order = noise * TOK_DEV + jnp.arange(TOK_DEV, dtype=jnp.int32)[None, None, :]
    ranked = jnp.argsort(order, axis=-1)
    return ranked[:, :, :SLOT].astype(jnp.int32)


def draw_counts(key, part):
    filled = jax.random.randint(jax.random.fold_in(key, 21), (OWNERS, EXPERTS), 1, SLOT + 1)
    fullest = jax.random.randint(jax.random.fold_in(key, 22), (EXPERTS,), 0, OWNERS)
    owner_ids = jnp.arange(OWNERS, dtype=jnp.int32)[:, None]
    return jnp.where(owner_ids == fullest[None, :], SLOT, filled).astype(jnp.int32)


def shard_levels(own_key, extent, cuts, least, high):
    level = 1.0
    for position, blocks in cuts:
        steps = jax.random.uniform(jax.random.fold_in(jax.random.fold_in(own_key, 6), position), (blocks,), jnp.float32, least / len(cuts), high / len(cuts))
        level = level * jnp.repeat(jnp.exp(steps), extent[position] // blocks).reshape((-1,) + (1,) * (len(extent) - 1 - position))
    return level


def centred(stream_key, extent, spread, bound, pieces=(), held_as=jnp.bfloat16):
    gain = shard_levels(stream_key, extent, pieces, -0.22, 0.18) if pieces else 1.0
    entries = jax.random.normal(stream_key, extent, jnp.float32) * spread * gain
    return jnp.minimum(jnp.maximum(entries, -bound), bound).astype(held_as)


def setup_inputs(seed: int = 0) -> dict:
    seeds = jax.random.split(jax.random.key(seed), 11)
    tokens = centred(seeds[0], (TOKENS, D), 1.0, 3.0, ((0, 128),))
    cotangent = centred(seeds[1], (TOKENS, D), 0.5, 2.0, ((0, 128),))
    router = centred(seeds[2], (D, EXPERTS), D ** -0.5, 0.09375)
    threshold = jnp.clip(jax.random.uniform(seeds[3], (EXPERTS,), jnp.float32, -1.0, 1.0), -1.0, 1.0)
    w_gate = centred(seeds[4], (EXPERTS, D, HID), D ** -0.5, 0.09375, ((0, 16), (2, 8)))
    w_up = centred(seeds[5], (EXPERTS, D, HID), D ** -0.5, 0.09375, ((0, 16), (2, 8)))
    w_down = centred(seeds[6], (EXPERTS, HID, D), HID ** -0.5, 0.15625, ((0, 16), (1, 8)))
    hid_scale = jnp.clip(jnp.exp(math.log(2.0) - 1.3862944 * jax.random.uniform(seeds[7], (EXPERTS, HID), jnp.float32) ** shard_levels(seeds[7], (EXPERTS, HID), ((0, 16), (1, 8)), -0.2, 0.2)), 0.5, 2.0)
    picks = draw_picks(jax.random.fold_in(seeds[10], 71), 0)
    counts = draw_counts(jax.random.fold_in(seeds[10], 71), 0)
    return dict(tokens=tokens, cotangent=cotangent, router=router, threshold=threshold, w_gate=w_gate, w_up=w_up, w_down=w_down, hid_scale=hid_scale, picks=picks, counts=counts)


def group_sum(left, right):
    group_size = left.shape[1] // N_SEQ
    left_parts = left.astype(jnp.float32).reshape(left.shape[0], N_SEQ, group_size)
    right_parts = right.astype(jnp.float32).reshape(N_SEQ, group_size, right.shape[1])
    parts = jnp.einsum("rsh,shd->rsd", left_parts, right_parts, precision=lax.Precision.HIGHEST)
    return jnp.sum(parts.astype(jnp.bfloat16).astype(jnp.float32), axis=1).astype(jnp.bfloat16)


def group_back(gate_delta, up_delta, gate_mat, up_mat):
    group_size = gate_delta.shape[1] // N_SEQ
    row_total = gate_delta.shape[0]
    gate_parts = gate_delta.astype(jnp.float32).reshape(row_total, N_SEQ, group_size)
    up_parts = up_delta.astype(jnp.float32).reshape(row_total, N_SEQ, group_size)
    gate_w = gate_mat.astype(jnp.float32).reshape(gate_mat.shape[0], N_SEQ, group_size)
    up_w = up_mat.astype(jnp.float32).reshape(up_mat.shape[0], N_SEQ, group_size)
    parts = jnp.einsum("rsh,dsh->rsd", gate_parts, gate_w, precision=lax.Precision.HIGHEST)
    parts = parts + jnp.einsum("rsh,dsh->rsd", up_parts, up_w, precision=lax.Precision.HIGHEST)
    return jnp.sum(parts.astype(jnp.bfloat16).astype(jnp.float32), axis=1).astype(jnp.bfloat16)


def reference(tokens, cotangent, router, threshold, w_gate, w_up, w_down, hid_scale, picks, counts):
    scores = jnp.dot(tokens, router, preferred_element_type=jnp.float32)
    gates = jax.nn.sigmoid(scores - threshold[None, :])
    owner_count = picks.shape[0]
    slot_count = picks.shape[2]
    expert_count = router.shape[1]
    owner_base = jnp.arange(owner_count, dtype=jnp.int32)[:, None] * TOK_DEV
    mixture = jnp.zeros(tokens.shape, jnp.float32)
    returned_sum = jnp.zeros(tokens.shape, jnp.float32)
    score_grad = jnp.zeros((tokens.shape[0], expert_count), jnp.float32)
    gate_list = []
    up_list = []
    down_list = []
    for expert in range(expert_count):
        row_index = (owner_base + picks[:, expert, :]).astype(jnp.int32).reshape(-1)
        active = (jnp.arange(slot_count, dtype=jnp.int32)[None, :] < counts[:, expert][:, None]).astype(jnp.float32).reshape(-1)
        exp_rows = tokens[row_index]
        raw_gate = gates[row_index, expert]
        gate_value = raw_gate * active
        cot_rows = cotangent[row_index].astype(jnp.float32)
        scaled_cot = (cot_rows * gate_value[:, None]).astype(jnp.bfloat16)
        pre_gate = jnp.dot(exp_rows, w_gate[expert], preferred_element_type=jnp.float32)
        pre_up = jnp.dot(exp_rows, w_up[expert], preferred_element_type=jnp.float32)
        sigmoid_val = jax.nn.sigmoid(pre_gate)
        activated = pre_gate * sigmoid_val
        hidden = (activated * pre_up * hid_scale[expert][None, :]).astype(jnp.bfloat16)
        expert_out = group_sum(hidden, w_down[expert])
        out_wide = expert_out.astype(jnp.float32)
        mixture = mixture.at[row_index].add(gate_value[:, None] * out_wide)
        hidden_grad = jnp.dot(scaled_cot, w_down[expert].T, preferred_element_type=jnp.float32)
        scaled_grad = hidden_grad * hid_scale[expert][None, :]
        gate_delta = (scaled_grad * pre_up * sigmoid_val * (1.0 + pre_gate * (1.0 - sigmoid_val))).astype(jnp.bfloat16)
        up_delta = (scaled_grad * activated).astype(jnp.bfloat16)
        down_list.append(jnp.dot(hidden.T, scaled_cot, preferred_element_type=jnp.float32))
        gate_list.append(jnp.dot(exp_rows.T, gate_delta, preferred_element_type=jnp.float32))
        up_list.append(jnp.dot(exp_rows.T, up_delta, preferred_element_type=jnp.float32))
        row_grad = group_back(gate_delta, up_delta, w_gate[expert], w_up[expert])
        returned_sum = returned_sum.at[row_index].add(row_grad.astype(jnp.float32))
        gate_pull = active * jnp.sum(cot_rows * out_wide, axis=-1)
        score_grad = score_grad.at[row_index, expert].add(gate_pull * raw_gate * (1.0 - raw_gate))
    token_grad = returned_sum + jnp.dot(score_grad, router.astype(jnp.float32).T, precision=lax.Precision.HIGHEST)
    router_grad = jnp.dot(tokens.astype(jnp.float32).T, score_grad, precision=lax.Precision.HIGHEST)
    threshold_grad = -jnp.sum(score_grad, axis=0)
    return (mixture.astype(jnp.bfloat16), token_grad.astype(jnp.bfloat16), router_grad, threshold_grad,
            jnp.stack(gate_list), jnp.stack(up_list), jnp.stack(down_list))
```

```python
import jax
import jax.numpy as jnp
from jax import lax
from jax.experimental import pallas as pl
from jax.experimental.pallas import tpu as pltpu
from jax.sharding import PartitionSpec as P

MESH = pl.DeviceIdType.MESH
BF = jnp.bfloat16
F32 = jnp.float32
HIGH = lax.Precision.HIGHEST
UP = (0, 2)
DOWN = (1, 3)


class Spot:
    def __init__(self):
        self.s = lax.axis_index("seq")
        self.e = lax.axis_index("exp")
        self.z = lax.div(self.s, 2)
        self.c = lax.rem(self.s, 2)
        self.y = lax.div(self.e, 4)
        self.x = lax.rem(self.e, 4)
        self.partner = (self.s + 1 - 2 * self.c, self.e)
        self.above = (self.layer(1) * 2 + self.c, self.e)
        self.below = (self.layer(3) * 2 + self.c, self.e)

    def layer(self, up):
        return lax.rem(self.z + up, 4)

    def group(self, i):
        return lax.rem(self.y + i, 4)

    def slot(self, up, other, i):
        core = self.c + other * (1 - 2 * self.c)
        return (self.layer(up) * 2 + core) * 4 + self.group(i)

    def plane_peers(self):
        return [(self.s, lax.rem(self.e + d, 16)) for d in range(1, 16)]

    def column_peers(self):
        return [(lax.rem(self.s + d, 8), self.e) for d in range(1, 8)]


def greet(peers):
    for peer in peers:
        pl.semaphore_signal(
            pltpu.get_barrier_semaphore(), inc=1, device_id=peer, device_id_type=MESH
        )


def greeted(count):
    pl.semaphore_wait(pltpu.get_barrier_semaphore(), count)


def push(src, dst, send_sem, recv_sem, device):
    copy = pltpu.make_async_remote_copy(
        src_ref=src,
        dst_ref=dst,
        send_sem=send_sem,
        recv_sem=recv_sem,
        device_id=device,
        device_id_type=MESH,
    )
    copy.start()
    return copy


def landed(dst, recv_sem, device):
    pltpu.make_async_remote_copy(
        src_ref=dst,
        dst_ref=dst,
        send_sem=recv_sem,
        recv_sem=recv_sem,
        device_id=device,
        device_id_type=MESH,
    ).wait_recv()


def dispatch_kernel(xr, cr, xc, msg, buf, s1, r1, sp, rp, sm, rm, sq, rq, own):
    at = Spot()
    peers = at.plane_peers()
    greet(peers + [at.partner, at.above, at.below])
    for e in range(16):
        msg[e, 0] = xr[4 * e : 4 * e + 4, :]
        msg[e, 1] = cr[4 * e : 4 * e + 4, :]
    greeted(18)
    sent = []
    for d, peer in enumerate(peers):
        sent.append(push(msg.at[peer[1]], buf.at[at.e], s1.at[d], r1.at[d], peer))
    mine = pltpu.make_async_copy(msg.at[at.e], buf.at[at.e], own)
    mine.start()
    mine.wait()

    def hand_over(slot, q):
        sent.append(push(xc.at[:, slot], xc.at[:, slot], sq.at[q], rq.at[q], at.partner))

    def climb(slot, k):
        sent.append(push(xc.at[:, slot], xc.at[:, slot], sp.at[k], rp.at[k], at.above))

    def sink(slot, k):
        sent.append(push(xc.at[:, slot], xc.at[:, slot], sm.at[k], rm.at[k], at.below))

    for i in range(4):
        group = at.group(i)
        slot = at.slot(0, 0, i)
        for x in range(4):
            origin = group * 4 + x
            behind = lax.rem(at.e - origin + 16, 16)

            @pl.when(behind > 0)
            def _():
                landed(buf.at[origin], r1.at[behind - 1], peers[0])

        for x in range(4):
            for a in range(2):
                xc[a, slot, 4 * x : 4 * x + 4, :] = buf[group * 4 + x, a]
        climb(slot, i)
        sink(slot, i)
        hand_over(slot, i)
    for i in range(4):
        slot = at.slot(3, 0, i)
        landed(xc.at[:, slot], rp.at[i], at.above)
        if i in UP:
            climb(slot, 4 + UP.index(i))
        hand_over(slot, 4 + i)
        slot = at.slot(1, 0, i)
        landed(xc.at[:, slot], rm.at[i], at.below)
        if i in DOWN:
            sink(slot, 4 + DOWN.index(i))
        hand_over(slot, 8 + i)
    for i in range(4):
        slot = at.slot(2, 0, i)
        if i in UP:
            landed(xc.at[:, slot], rp.at[4 + UP.index(i)], at.above)
        else:
            landed(xc.at[:, slot], rm.at[4 + DOWN.index(i)], at.below)
        hand_over(slot, 12 + i)
    for q in range(16):
        up = (0, 3, 1, 2)[q // 4]
        landed(xc.at[:, at.slot(up, 1, q % 4)], rq.at[q], at.partner)
    for copy in sent:
        copy.wait_send()


def dispatch(rows, cots):
    width = rows.shape[1]
    vmem = pl.BlockSpec(memory_space=pltpu.VMEM)
    dma = pltpu.SemaphoreType.DMA
    return pl.pallas_call(
        dispatch_kernel,
        out_shape=jax.ShapeDtypeStruct((2, 32, 16, width), BF),
        in_specs=[vmem, vmem],
        out_specs=vmem,
        scratch_shapes=[
            pltpu.VMEM((16, 2, 4, width), BF),
            pltpu.VMEM((16, 2, 4, width), BF),
            dma((15,)), dma((15,)), dma((6,)), dma((6,)), dma((6,)), dma((6,)),
            dma((16,)), dma((16,)), dma,
        ],
        compiler_params=pltpu.CompilerParams(
            collective_id=0, has_side_effects=True, vmem_limit_bytes=60 << 20
        ),
    )(rows, cots)


def total(dst, parts):
    width = parts[0].shape[-1]
    step = 512

    def body(j, carry):
        cols = pl.ds(pl.multiple_of(j * step, step), step)
        acc = parts[0][:, :, cols].astype(F32)
        for part in parts[1:]:
            acc = acc + part[:, :, cols].astype(F32)
        dst[:, :, cols] = acc.astype(BF)
        return carry

    lax.fori_loop(0, width // step, body, 0)


def return_kernel(
    p, ret, pb, xp, xm, tot, om, rb, sq, rq, sp, rp, sm, rm, s3, r3, own
):
    at = Spot()
    peers = at.plane_peers()
    greet(peers + [at.partner, at.above, at.below])
    greeted(18)
    order = (
        [(1, i) for i in DOWN] + [(3, i) for i in UP] + [(2, i) for i in range(4)]
        + [(1, i) for i in UP] + [(3, i) for i in DOWN] + [(0, i) for i in range(4)]
    )
    sent = []
    for up, i in order:
        q = up * 4 + i
        slot = at.slot(up, 1, i)
        sent.append(push(p.at[:, slot], pb.at[q], sq.at[q], rq.at[q], at.partner))

    def climb(src, k):
        sent.append(push(src, xp.at[k], sp.at[k], rp.at[k], at.above))

    def sink(src, k):
        sent.append(push(src, xm.at[k], sm.at[k], rm.at[k], at.below))

    for up, i in order:
        q = up * 4 + i
        slot = at.slot(up, 0, i)
        landed(pb.at[q], rq.at[q], at.partner)
        parts = [p.at[:, slot], pb.at[q]]
        if up == 1 and i in UP:
            k = 2 + UP.index(i)
            landed(xp.at[k], rp.at[k], at.above)
            parts.append(xp.at[k])
        if up == 3 and i in DOWN:
            k = 2 + DOWN.index(i)
            landed(xm.at[k], rm.at[k], at.below)
            parts.append(xm.at[k])
        if up == 0:
            ku = UP.index(i) + 4 if i in UP else DOWN.index(i)
            kd = UP.index(i) if i in UP else DOWN.index(i) + 4
            landed(xp.at[ku], rp.at[ku], at.above)
            landed(xm.at[kd], rm.at[kd], at.below)
            parts += [xp.at[ku], xm.at[kd]]
        total(tot.at[q], parts)
        if up == 1:
            climb(tot.at[q], UP.index(i) + 4 if i in UP else DOWN.index(i))
        if up == 3:
            sink(tot.at[q], UP.index(i) if i in UP else DOWN.index(i) + 4)
        if up == 2:
            if i in UP:
                climb(tot.at[q], 2 + UP.index(i))
            else:
                sink(tot.at[q], 2 + DOWN.index(i))
        if up == 0:
            group = at.group(i)
            for x in range(4):
                for a in range(2):
                    om[i * 4 + x, a] = tot[q, a, 4 * x : 4 * x + 4, :]
            for x in range(4):
                m = i * 4 + x
                target = group * 4 + x
                ahead = lax.rem(target - at.e + 16, 16)

                def go():
                    return pltpu.make_async_remote_copy(
                        src_ref=om.at[m],
                        dst_ref=rb.at[at.e],
                        send_sem=s3.at[m],
                        recv_sem=r3.at[ahead - 1],
                        device_id=(at.s, target),
                        device_id_type=MESH,
                    )

                @pl.when(ahead > 0)
                def _():
                    go().start()

                @pl.when(ahead == 0)
                def _():
                    mine = pltpu.make_async_copy(om.at[m], rb.at[at.e], own)
                    mine.start()
                    mine.wait()

    for e in range(16):
        behind = lax.rem(at.e - e + 16, 16)

        @pl.when(behind > 0)
        def _():
            landed(rb.at[e], r3.at[behind - 1], peers[0])

        for a in range(2):
            ret[a, 4 * e : 4 * e + 4, :] = rb[e, a]
    for i in range(4):
        for x in range(4):
            m = i * 4 + x
            target = at.group(i) * 4 + x
            ahead = lax.rem(target - at.e + 16, 16)

            @pl.when(ahead > 0)
            def _():
                pltpu.make_async_remote_copy(
                    src_ref=om.at[m],
                    dst_ref=rb.at[at.e],
                    send_sem=s3.at[m],
                    recv_sem=r3.at[ahead - 1],
                    device_id=(at.s, target),
                    device_id_type=MESH,
                ).wait_send()

    for copy in sent:
        copy.wait_send()


def give_back(parts):
    width = parts.shape[-1]
    vmem = pl.BlockSpec(memory_space=pltpu.VMEM)
    dma = pltpu.SemaphoreType.DMA
    return pl.pallas_call(
        return_kernel,
        out_shape=jax.ShapeDtypeStruct((2, 64, width), BF),
        in_specs=[vmem],
        out_specs=vmem,
        scratch_shapes=[
            pltpu.VMEM((16, 2, 16, width), BF),
            pltpu.VMEM((6, 2, 16, width), BF),
            pltpu.VMEM((6, 2, 16, width), BF),
            pltpu.VMEM((16, 2, 16, width), BF),
            pltpu.VMEM((16, 2, 4, width), BF),
            pltpu.VMEM((16, 2, 4, width), BF),
            dma((16,)), dma((16,)), dma((6,)), dma((6,)), dma((6,)), dma((6,)),
            dma((16,)), dma((15,)), dma,
        ],
        compiler_params=pltpu.CompilerParams(
            collective_id=1, has_side_effects=True, vmem_limit_bytes=60 << 20
        ),
    )(parts)


def reduce_kernel(t, out, a, b, ext, sa, ra, sb, rb):
    at = Spot()
    column = at.column_peers()
    plane = at.plane_peers()
    greet(column + plane)
    greeted(22)
    sent = []
    for d, peer in enumerate(column):
        sent.append(push(t.at[peer[0]], a.at[d], sa.at[d], ra.at[d], peer))
    acc = t[at.s]
    for d in range(7):
        landed(a.at[d], ra.at[d], column[d])
        acc = acc + a[d]
    for y in range(4):
        ext[y, 0:16, :] = acc[0:16, 128 * y : 128 * y + 128]
        ext[y, 16:24, :] = acc[16:24, 0:128]
    for d, peer in enumerate(plane):
        sent.append(push(ext.at[lax.div(peer[1], 4)], b.at[d], sb.at[d], rb.at[d], peer))
    done = ext[at.y]
    th = done[16:24, :]
    res = done[0:16, :]
    for d in range(15):
        landed(b.at[d], rb.at[d], plane[d])
        res = res + b[d, 0:16, :]
        th = th + b[d, 16:24, :]
    out[0:16, :] = res
    out[16:24, :] = th
    for copy in sent:
        copy.wait_send()


def reduce_all(t):
    vmem = pl.BlockSpec(memory_space=pltpu.VMEM)
    dma = pltpu.SemaphoreType.DMA
    return pl.pallas_call(
        reduce_kernel,
        out_shape=jax.ShapeDtypeStruct((24, 128), F32),
        in_specs=[vmem],
        out_specs=vmem,
        scratch_shapes=[
            pltpu.VMEM((7, 24, 512), F32),
            pltpu.VMEM((15, 24, 128), F32),
            pltpu.VMEM((4, 24, 128), F32),
            dma((7,)), dma((7,)), dma((15,)), dma((15,)),
        ],
        compiler_params=pltpu.CompilerParams(collective_id=2, has_side_effects=True),
    )(t)


def on_device(tokens, cotangent, router, threshold, w_gate, w_up, w_down, hid_scale, picks, counts):
    experts = router.shape[1]
    slot_count = picks.shape[2]
    features = tokens.shape[1]
    row_count = tokens.shape[0]
    chosen = picks[0]
    active = (jnp.arange(slot_count, dtype=jnp.int32)[None, :] < counts[0][:, None]).astype(F32)
    scores = jnp.dot(tokens, router, preferred_element_type=F32)
    gates_all = jax.nn.sigmoid(scores - threshold[None, :])
    select = (
        chosen.reshape(-1)[:, None] == jnp.arange(row_count, dtype=jnp.int32)[None, :]
    )
    select_bf = select.astype(BF)
    select_f = select.astype(F32)
    gates_wide = jnp.repeat(gates_all.T, slot_count, axis=0)
    raw_gate = jnp.sum(jnp.where(select, gates_wide, 0.0), axis=1)
    live = active.reshape(-1)
    gate_value = raw_gate * live
    picked_rows = jnp.dot(select_bf, tokens, preferred_element_type=F32).astype(BF)
    picked_cot = jnp.dot(select_bf, cotangent, preferred_element_type=F32)
    scaled_cot = (picked_cot * gate_value[:, None]).astype(BF)
    arrived = dispatch(picked_rows, scaled_cot)
    expert_rows = arrived[0].reshape(-1, features)
    expert_cot = arrived[1].reshape(-1, features)
    gate_mat = w_gate[0]
    up_mat = w_up[0]
    down_mat = w_down[0]
    scale_row = hid_scale[0][None, :]
    pre_gate = jnp.dot(expert_rows, gate_mat, preferred_element_type=F32)
    pre_up = jnp.dot(expert_rows, up_mat, preferred_element_type=F32)
    sigmoid_val = jax.nn.sigmoid(pre_gate)
    activated = pre_gate * sigmoid_val
    hidden = (activated * pre_up * scale_row).astype(BF)
    scaled_grad = jnp.dot(expert_cot, down_mat.T, preferred_element_type=F32) * scale_row
    gate_delta = (
        scaled_grad * pre_up * sigmoid_val * (1.0 + pre_gate * (1.0 - sigmoid_val))
    ).astype(BF)
    up_delta = (scaled_grad * activated).astype(BF)
    contract_rows = (((0,), (0,)), ((), ()))
    down_grad = lax.dot_general(hidden, expert_cot, contract_rows, preferred_element_type=F32)
    gate_grad = lax.dot_general(expert_rows, gate_delta, contract_rows, preferred_element_type=F32)
    up_grad = lax.dot_general(expert_rows, up_delta, contract_rows, preferred_element_type=F32)
    part_out = jnp.dot(hidden, down_mat, preferred_element_type=F32).astype(BF)
    contract_hidden = (((1,), (1,)), ((), ()))
    part_grad = (
        lax.dot_general(gate_delta, gate_mat, contract_hidden, preferred_element_type=F32)
        + lax.dot_general(up_delta, up_mat, contract_hidden, preferred_element_type=F32)
    ).astype(BF)
    returned = give_back(jnp.stack([part_out, part_grad]).reshape(2, 32, 16, features))
    out_wide = returned[0].astype(F32)
    mixture = lax.dot_general(
        select_f * gate_value[:, None], out_wide, contract_rows, precision=HIGH
    )
    gate_pull = live * jnp.sum(picked_cot * out_wide, axis=-1)
    score_pick = gate_pull * raw_gate * (1.0 - raw_gate)
    by_row = select_f * score_pick[:, None]
    score_grad_t = jnp.sum(by_row.reshape(experts, slot_count, row_count), axis=1)
    token_grad = lax.dot_general(
        select_bf, returned[1], contract_rows, preferred_element_type=F32
    )
    token_grad = token_grad + lax.dot_general(
        score_grad_t, router.astype(F32).T, contract_rows, precision=HIGH
    )
    router_term = jnp.dot(score_grad_t, tokens.astype(F32), precision=HIGH)
    bias_term = jnp.sum(score_grad_t, axis=1)
    bias_tile = jnp.broadcast_to(
        jnp.pad(bias_term, (0, 512 - experts))[None, None, :], (8, 8, 512)
    )
    pieces = router_term.reshape(experts, 8, 512).transpose(1, 0, 2)
    reduced = reduce_all(jnp.concatenate([pieces, bias_tile], axis=1))
    quarter = lax.rem(lax.axis_index("exp"), 4)
    router_grad = lax.dynamic_slice(reduced, (0, quarter * 32), (experts, 32)).T
    threshold_grad = -reduced[16, :experts]
    return (
        mixture.astype(BF),
        token_grad.astype(BF),
        router_grad,
        threshold_grad,
        gate_grad[None],
        up_grad[None],
        down_grad[None],
    )


def solution(mesh):
    placed = (
        P(("seq", "exp"), None),
        P(("seq", "exp"), None),
        P(),
        P(),
        P("exp", None, "seq"),
        P("exp", None, "seq"),
        P("exp", "seq", None),
        P("exp", "seq"),
        P(("seq", "exp"), None, None),
        P(("seq", "exp"), None),
    )
    return jax.shard_map(
        on_device,
        mesh=mesh,
        in_specs=placed,
        out_specs=(
            P(("seq", "exp"), None),
            P(("seq", "exp"), None),
            P(("seq", "exp"), None),
            P(),
            P("exp", None, "seq"),
            P("exp", None, "seq"),
            P("exp", "seq", None),
        ),
        check_vma=False,
    )
```

```python
import jax
import jax.numpy as jnp
from jax import lax
from jax.experimental import pallas as pl
from jax.experimental.pallas import tpu as pltpu
from jax.sharding import PartitionSpec as P

MESH = pl.DeviceIdType.MESH
BF = jnp.bfloat16
F32 = jnp.float32
HIGH = lax.Precision.HIGHEST
UP = (0, 2)
DOWN = (1, 3)


class Spot:
    def __init__(self):
        self.s = lax.axis_index("seq")
        self.e = lax.axis_index("exp")
        self.z = lax.div(self.s, 2)
        self.c = lax.rem(self.s, 2)
        self.y = lax.div(self.e, 4)
        self.x = lax.rem(self.e, 4)
        self.partner = (self.s + 1 - 2 * self.c, self.e)
        self.above = (self.layer(1) * 2 + self.c, self.e)
        self.below = (self.layer(3) * 2 + self.c, self.e)

    def layer(self, up):
        return lax.rem(self.z + up, 4)

    def group(self, i):
        return lax.rem(self.y + i, 4)

    def slot(self, up, other, i):
        core = self.c + other * (1 - 2 * self.c)
        return (self.layer(up) * 2 + core) * 4 + self.group(i)

    def in_plane(self, i, j):
        return lax.rem(self.y + i, 4) * 4 + lax.rem(self.x + j, 4)

    def plane_peers(self):
        return [(self.s, lax.rem(self.e + d, 16)) for d in range(1, 16)]

    def column_peers(self):
        return [(lax.rem(self.s + d, 8), self.e) for d in range(1, 8)]


def greet(peers):
    for peer in peers:
        pl.semaphore_signal(
            pltpu.get_barrier_semaphore(), inc=1, device_id=peer, device_id_type=MESH
        )


def greeted(count):
    pl.semaphore_wait(pltpu.get_barrier_semaphore(), count)


def push(src, dst, send_sem, recv_sem, device):
    copy = pltpu.make_async_remote_copy(
        src_ref=src,
        dst_ref=dst,
        send_sem=send_sem,
        recv_sem=recv_sem,
        device_id=device,
        device_id_type=MESH,
    )
    copy.start()
    return copy


def landed(dst, recv_sem, device):
    pltpu.make_async_remote_copy(
        src_ref=dst,
        dst_ref=dst,
        send_sem=recv_sem,
        recv_sem=recv_sem,
        device_id=device,
        device_id_type=MESH,
    ).wait_recv()


HOPS = [(i, j) for i in range(4) for j in (0, 1, 3, 2)]
NT = (((1,), (1,)), ((), ()))
TN = (((0,), (0,)), ((), ()))


def dot(a, b):
    return jnp.dot(a, b, preferred_element_type=F32)


def thirds(v):
    first = v.astype(BF)
    rest = v - first.astype(F32)
    second = rest.astype(BF)
    return first, second, (rest - second.astype(F32)).astype(BF)


def tiles(count, width, body):
    def step(j, carry):
        body(j, pl.ds(pl.multiple_of(j * width, width), width))
        return carry

    lax.fori_loop(0, count, step, 0)


def layer_kernel(
    tok_h, cot_h, wg_h, wu_h, wd_h, router, thr, scale, meta,
    mix_h, tgr_h, rows_h, red, hid, gdel, udel,
    tok, cot, wg, wu, wd, xr, cr, pc, msg, buf, xc, pp, pb, tot, xp, xm, om, rb, ret,
    pre_g, pre_u, hg, base, mix, tgr, t, ta, ext, tb,
    s1, r1, sp, rp, sm, rm, sq, rq, es, er, tps, tpr, tms, tmr, s3, r3, sa, ra, sb, rbs, loc,
):
    at = Spot()
    plane = at.plane_peers()
    column = at.column_peers()
    greet(plane + column)
    loads = [
        pltpu.make_async_copy(a, b, loc.at[k])
        for k, (a, b) in enumerate(
            [(tok_h, tok), (cot_h, cot), (wg_h, wg), (wu_h, wu), (wd_h, wd)]
        )
    ]
    for load in loads:
        load.start()

    pick = meta[:, 0:1]
    live = meta[:, 1:2].astype(F32)
    select = (pick == lax.broadcasted_iota(jnp.int32, (64, 256), 1)).astype(F32)
    select_bf = select.astype(BF)
    mine16 = (
        lax.div(lax.broadcasted_iota(jnp.int32, (64, 16), 0), 4)
        == lax.broadcasted_iota(jnp.int32, (64, 16), 1)
    ).astype(F32)
    loads[0].wait()
    gates = jax.nn.sigmoid(dot(tok[...], router[...]) - thr[...])
    chosen_gates = jnp.dot(select, gates, precision=HIGH, preferred_element_type=F32)
    raw = jnp.sum(chosen_gates * mine16, axis=1, keepdims=True)
    gate = raw * live

    def take_rows(j, cols):
        xr[:, cols] = dot(select_bf, tok[:, cols]).astype(BF)

    tiles(8, 512, take_rows)
    loads[1].wait()

    def take_cots(j, cols):
        cots = dot(select_bf, cot[:, cols])
        pc[:, cols] = cots.astype(BF)
        cr[:, cols] = (cots * gate).astype(BF)

    tiles(8, 512, take_cots)
    for e in range(16):
        msg[e, 0] = xr[4 * e : 4 * e + 4, :]
        msg[e, 1] = cr[4 * e : 4 * e + 4, :]
    greeted(22)

    sent = []
    own = pltpu.make_async_copy(msg.at[at.e], buf.at[at.e], loc.at[5])
    own.start()
    for i, j in HOPS:
        if i or j:
            e = at.in_plane(4 - i, j)
            k = i * 4 + j
            sent.append(push(msg.at[e], buf.at[at.e], s1.at[k], r1.at[k], (at.s, e)))
    own.wait()

    def hand_over(slot, q):
        sent.append(push(xc.at[:, slot], xc.at[:, slot], sq.at[q], rq.at[q], at.partner))

    def climb(slot, k):
        sent.append(push(xc.at[:, slot], xc.at[:, slot], sp.at[k], rp.at[k], at.above))

    def sink(slot, k):
        sent.append(push(xc.at[:, slot], xc.at[:, slot], sm.at[k], rm.at[k], at.below))

    for i in range(4):
        group = at.group(i)
        slot = at.slot(0, 0, i)
        for j in range(4):
            if i or j:
                landed(buf.at[at.in_plane(i, 4 - j)], r1.at[i * 4 + j], at.partner)
        for x in range(4):
            for a in range(2):
                xc[a, slot, 4 * x : 4 * x + 4, :] = buf[group * 4 + x, a]
        climb(slot, i)
        sink(slot, i)
        hand_over(slot, i)

    def from_beside(i):
        slot = at.slot(3, 0, i)
        landed(xc.at[:, slot], rp.at[i], at.above)
        if i in UP:
            climb(slot, 4 + UP.index(i))
        hand_over(slot, 4 + i)
        slot = at.slot(1, 0, i)
        landed(xc.at[:, slot], rm.at[i], at.below)
        if i in DOWN:
            sink(slot, 4 + DOWN.index(i))
        hand_over(slot, 8 + i)

    def from_across(i):
        slot = at.slot(2, 0, i)
        if i in UP:
            landed(xc.at[:, slot], rp.at[4 + UP.index(i)], at.above)
        else:
            landed(xc.at[:, slot], rm.at[4 + DOWN.index(i)], at.below)
        hand_over(slot, 12 + i)

    def from_partner(up):
        first = (0, 8, 12, 4)[up]
        for i in range(4):
            landed(xc.at[:, at.slot(up, 1, i)], rq.at[first + i], at.partner)

    def forward(up):
        lay = at.layer(up)
        slots = pl.ds(lay * 8, 8)
        pre_g[lay] = jnp.zeros_like(pre_g[lay])
        pre_u[lay] = jnp.zeros_like(pre_u[lay])

        def before(j, cols):
            a = xc[0, slots, :, cols].reshape(128, 1024)
            pre_g[lay] += dot(a, wg[cols, :])
            pre_u[lay] += dot(a, wu[cols, :])

        tiles(4, 1024, before)
        g = pre_g[lay]
        h = (g * jax.nn.sigmoid(g) * pre_u[lay] * scale[...]).astype(BF)
        hid[lay] = h

        def after(j, cols):
            pp[0, slots, :, cols] = dot(h, wd[:, cols]).astype(BF).reshape(8, 16, 512)

        tiles(8, 512, after)

    def backward(up):
        lay = at.layer(up)
        slots = pl.ds(lay * 8, 8)
        hg[...] = jnp.zeros_like(hg)

        def before(j, cols):
            a = xc[1, slots, :, cols].reshape(128, 1024)
            hg[...] += lax.dot_general(a, wd[:, cols], NT, preferred_element_type=F32)

        tiles(4, 1024, before)
        g = pre_g[lay]
        sig = jax.nn.sigmoid(g)
        grad = hg[...] * scale[...]
        gd = (grad * pre_u[lay] * sig * (1.0 + g * (1.0 - sig))).astype(BF)
        ud = (grad * (g * sig)).astype(BF)
        gdel[lay] = gd
        udel[lay] = ud

        def after(j, cols):
            v = lax.dot_general(gd, wg[cols, :], NT, preferred_element_type=F32)
            v = v + lax.dot_general(ud, wu[cols, :], NT, preferred_element_type=F32)
            pp[1, slots, :, cols] = v.astype(BF).reshape(8, 16, 512)

        tiles(8, 512, after)

    def trade(kind, up):
        slots = pl.ds(at.slot(up, 1, 0) - at.y, 4)
        sent.append(
            push(pp.at[kind, slots], pb.at[kind, up], es.at[kind, up], er.at[kind, up], at.partner)
        )

    def traded(kind, up):
        landed(pb.at[kind, up], er.at[kind, up], at.partner)

    def combine(kind, up, i, extra):
        q = up * 4 + i
        parts = [pp.at[kind, at.slot(up, 0, i)], pb.at[kind, up, at.group(i)]] + extra

        def add(j, cols):
            acc = parts[0][:, cols].astype(F32)
            for part in parts[1:]:
                acc = acc + part[:, cols].astype(F32)
            tot[kind, q, :, cols] = acc.astype(BF)

        tiles(4, 1024, add)
        return tot.at[kind, q]

    def up_send(kind, src, k):
        sent.append(push(src, xp.at[kind, k], tps.at[kind, k], tpr.at[kind, k], at.above))

    def down_send(kind, src, k):
        sent.append(push(src, xm.at[kind, k], tms.at[kind, k], tmr.at[kind, k], at.below))

    def from_below(kind, k):
        landed(xp.at[kind, k], tpr.at[kind, k], at.above)
        return xp.at[kind, k]

    def from_above(kind, k):
        landed(xm.at[kind, k], tmr.at[kind, k], at.below)
        return xm.at[kind, k]

    def send_plain(kind):
        for k in range(2):
            up_send(kind, combine(kind, 1, DOWN[k], []), k)
            down_send(kind, combine(kind, 3, UP[k], []), k)

    def send_across(kind):
        for k in range(2):
            up_send(kind, combine(kind, 2, UP[k], []), 2 + k)
            down_send(kind, combine(kind, 2, DOWN[k], []), 2 + k)

    def send_merged(kind):
        for k in range(2):
            up_send(kind, combine(kind, 1, UP[k], [from_below(kind, 2 + k)]), 4 + k)
            down_send(kind, combine(kind, 3, DOWN[k], [from_above(kind, 2 + k)]), 4 + k)

    def send_home(kind):
        for i in (1, 0, 3, 2):
            k = i // 2
            if i in UP:
                extra = [from_above(kind, k), from_below(kind, 4 + k)]
            else:
                extra = [from_below(kind, k), from_above(kind, 4 + k)]
            sums = combine(kind, 0, i, extra)
            for x in range(4):
                om[kind, i * 4 + x] = sums[4 * x : 4 * x + 4, :]
            for j in (1, 3, 2, 0):
                e = at.in_plane(i, j)
                src = om.at[kind, i * 4 + lax.rem(at.x + j, 4)]
                k = i * 4 + j
                if k:
                    sent.append(
                        push(src, rb.at[kind, at.e], s3.at[kind, k], r3.at[kind, k], (at.s, e))
                    )
                else:
                    pltpu.make_async_copy(src, rb.at[kind, at.e], loc.at[6 + kind]).start()

    def came_home(kind):
        for i, j in HOPS:
            e = at.in_plane(4 - i, 4 - j)
            if i or j:
                landed(rb.at[kind, e], r3.at[kind, i * 4 + j], at.partner)
            else:
                pltpu.make_async_copy(om.at[kind, at.x], rb.at[kind, e], loc.at[6 + kind]).wait()
        for e in range(16):
            ret[kind, 4 * e : 4 * e + 4, :] = rb[kind, e]

    for load in loads[2:]:
        load.wait()
    from_beside(0)
    from_partner(0)
    forward(0)
    from_beside(1)
    backward(0)
    trade(0, 0)
    trade(1, 0)
    from_beside(2)
    from_beside(3)
    from_partner(3)
    forward(3)
    trade(0, 3)
    from_partner(1)
    forward(1)
    trade(0, 1)
    from_across(0)
    from_across(1)
    traded(0, 3)
    traded(0, 1)
    send_plain(0)
    backward(3)
    trade(1, 3)
    backward(1)
    trade(1, 1)
    from_across(2)
    from_across(3)
    from_partner(2)
    forward(2)
    trade(0, 2)
    rows_out = pltpu.make_async_copy(xc, rows_h, loc.at[8])
    rows_out.start()
    traded(1, 3)
    traded(1, 1)
    traded(0, 2)
    send_across(0)
    send_plain(1)
    backward(2)
    trade(1, 2)
    send_merged(0)
    traded(1, 2)
    send_across(1)
    traded(0, 0)
    send_home(0)
    send_merged(1)
    came_home(0)

    pulls = jnp.zeros((64, 1), F32)
    for j in range(4):
        cols = slice(1024 * j, 1024 * j + 1024)
        pulls = pulls + jnp.sum(
            pc[:, cols].astype(F32) * ret[0, :, cols].astype(F32), axis=1, keepdims=True
        )
    score = live * pulls * raw * (1.0 - raw)
    by_row = select * score
    sgt = lax.dot_general(mine16, by_row, TN, precision=HIGH, preferred_element_type=F32)
    sg = lax.dot_general(by_row, mine16, TN, precision=HIGH, preferred_element_type=F32)
    parts = jnp.concatenate([v.astype(F32) for v in thirds(sgt)], axis=0).astype(BF)
    bias = jnp.broadcast_to(jnp.sum(sgt, axis=1, keepdims=True), (16, 512))

    def router_tile(j, cols):
        v = dot(parts, tok[:, cols])
        t[j, 0:16, :] = v[0:16] + v[16:32] + v[32:48]
        t[j, 16:32, :] = bias

    tiles(8, 512, router_tile)
    for d, peer in enumerate(column):
        sent.append(push(t.at[peer[0]], ta.at[d], sa.at[d], ra.at[d], peer))

    mix_parts = [w.T for w in (select * gate,)]
    w1, w2, w3 = thirds(mix_parts[0])
    sg1, sg2, sg3 = thirds(sg)

    def mix_tile(j, cols):
        rows = ret[0, :, cols]
        mix[:, cols] = (dot(w1, rows) + dot(w2, rows) + dot(w3, rows)).astype(BF)
        r = router[cols, :]
        v = lax.dot_general(sg1, r, NT, preferred_element_type=F32)
        v = v + lax.dot_general(sg2, r, NT, preferred_element_type=F32)
        base[:, cols] = v + lax.dot_general(sg3, r, NT, preferred_element_type=F32)

    tiles(8, 512, mix_tile)
    mix_out = pltpu.make_async_copy(mix, mix_h, loc.at[9])
    mix_out.start()

    acc = t[at.s]
    for d in range(7):
        landed(ta.at[d], ra.at[d], at.partner)
        acc = acc + ta[d]
    for y in range(4):
        ext[y, 0:16, :] = acc[0:16, 128 * y : 128 * y + 128]
        ext[y, 16:32, :] = acc[16:32, 0:128]
    for d, peer in enumerate(plane):
        sent.append(push(ext.at[lax.div(peer[1], 4)], tb.at[d], sb.at[d], rbs.at[d], peer))

    traded(1, 0)
    send_home(1)
    done = ext[at.y]
    for d in range(15):
        landed(tb.at[d], rbs.at[d], at.partner)
        done = done + tb[d]
    red[...] = done
    came_home(1)
    select_t = select.T.astype(BF)

    def grad_tile(j, cols):
        tgr[:, cols] = (base[:, cols] + dot(select_t, ret[1, :, cols])).astype(BF)

    tiles(8, 512, grad_tile)
    grad_out = pltpu.make_async_copy(tgr, tgr_h, loc.at[10])
    grad_out.start()
    for copy in sent:
        copy.wait_send()
    rows_out.wait()
    mix_out.wait()
    grad_out.wait()


def layer(tokens, cotangent, wg, wu, wd, router, thr, scale, meta):
    vmem = pl.BlockSpec(memory_space=pltpu.VMEM)
    hbm = pl.BlockSpec(memory_space=pl.ANY)
    dma = pltpu.SemaphoreType.DMA
    v = pltpu.VMEM
    width = tokens.shape[1]
    units = wg.shape[1]
    shape = jax.ShapeDtypeStruct
    return pl.pallas_call(
        layer_kernel,
        out_shape=(
            shape((256, width), BF),
            shape((256, width), BF),
            shape((2, 32, 16, width), BF),
            shape((32, 128), F32),
            shape((4, 128, units), BF),
            shape((4, 128, units), BF),
            shape((4, 128, units), BF),
        ),
        in_specs=[hbm] * 5 + [vmem] * 4,
        out_specs=(hbm, hbm, hbm, vmem, vmem, vmem, vmem),
        scratch_shapes=[
            v((256, width), BF), v((256, width), BF),
            v((width, units), BF), v((width, units), BF), v((units, width), BF),
            v((64, width), BF), v((64, width), BF), v((64, width), BF),
            v((16, 2, 4, width), BF), v((16, 2, 4, width), BF),
            v((2, 32, 16, width), BF), v((2, 32, 16, width), BF),
            v((2, 4, 4, 16, width), BF), v((2, 16, 16, width), BF),
            v((2, 6, 16, width), BF), v((2, 6, 16, width), BF),
            v((2, 16, 4, width), BF), v((2, 16, 4, width), BF), v((2, 64, width), BF),
            v((4, 128, units), F32), v((4, 128, units), F32), v((128, units), F32),
            v((256, width), F32), v((256, width), BF), v((256, width), BF),
            v((8, 32, 512), F32), v((7, 32, 512), F32), v((4, 32, 128), F32),
            v((15, 32, 128), F32),
            dma((16,)), dma((16,)), dma((6,)), dma((6,)), dma((6,)), dma((6,)),
            dma((16,)), dma((16,)), dma((2, 4)), dma((2, 4)),
            dma((2, 6)), dma((2, 6)), dma((2, 6)), dma((2, 6)),
            dma((2, 16)), dma((2, 16)), dma((7,)), dma((7,)), dma((15,)), dma((15,)),
            dma((11,)),
        ],
        compiler_params=pltpu.CompilerParams(
            collective_id=0, has_side_effects=True, vmem_limit_bytes=67043328
        ),
    )(tokens, cotangent, wg, wu, wd, router, thr, scale, meta)


def on_device(tokens, cotangent, router, threshold, w_gate, w_up, w_down, hid_scale, picks, counts):
    experts = router.shape[1]
    slot_count = picks.shape[2]
    features = tokens.shape[1]
    active = jnp.arange(slot_count, dtype=jnp.int32)[None, :] < counts[0][:, None]
    meta = jnp.stack([picks[0], active.astype(jnp.int32)], axis=-1).reshape(-1, 2)
    mixture, token_grad, rows, reduced, hidden, gate_delta, up_delta = layer(
        tokens, cotangent, w_gate[0], w_up[0], w_down[0], router,
        threshold[None, :], hid_scale[0][None, :], meta,
    )
    expert_rows = rows[0].reshape(-1, features)
    expert_cot = rows[1].reshape(-1, features)
    flat = (expert_rows.shape[0], -1)
    down_grad = lax.dot_general(
        hidden.reshape(flat), expert_cot, TN, preferred_element_type=F32
    )
    gate_grad = lax.dot_general(
        expert_rows, gate_delta.reshape(flat), TN, preferred_element_type=F32
    )
    up_grad = lax.dot_general(
        expert_rows, up_delta.reshape(flat), TN, preferred_element_type=F32
    )
    quarter = lax.rem(lax.axis_index("exp"), 4)
    router_grad = lax.dynamic_slice(reduced, (0, quarter * 32), (experts, 32)).T
    threshold_grad = -reduced[experts : 2 * experts, 0]
    return (
        mixture,
        token_grad,
        router_grad,
        threshold_grad,
        gate_grad[None],
        up_grad[None],
        down_grad[None],
    )


def solution(mesh):
    placed = (
        P(("seq", "exp"), None),
        P(("seq", "exp"), None),
        P(),
        P(),
        P("exp", None, "seq"),
        P("exp", None, "seq"),
        P("exp", "seq", None),
        P("exp", "seq"),
        P(("seq", "exp"), None, None),
        P(("seq", "exp"), None),
    )
    return jax.shard_map(
        on_device,
        mesh=mesh,
        in_specs=placed,
        out_specs=(
            P(("seq", "exp"), None),
            P(("seq", "exp"), None),
            P(("seq", "exp"), None),
            P(),
            P("exp", None, "seq"),
            P("exp", None, "seq"),
            P("exp", "seq", None),
        ),
        check_vma=False,
    )
```

```python
import jax
import jax.numpy as jnp
from jax import lax
from jax.experimental import pallas as pl
from jax.experimental.pallas import tpu as pltpu
from jax.sharding import PartitionSpec as P

MESH = pl.DeviceIdType.MESH
BF = jnp.bfloat16
F32 = jnp.float32
HIGH = lax.Precision.HIGHEST
UP = (0, 2)
DOWN = (1, 3)


class Spot:
    def __init__(self):
        self.s = lax.axis_index("seq")
        self.e = lax.axis_index("exp")
        self.z = lax.div(self.s, 2)
        self.c = lax.rem(self.s, 2)
        self.y = lax.div(self.e, 4)
        self.x = lax.rem(self.e, 4)
        self.partner = (self.s + 1 - 2 * self.c, self.e)
        self.above = (self.layer(1) * 2 + self.c, self.e)
        self.below = (self.layer(3) * 2 + self.c, self.e)

    def layer(self, up):
        return lax.rem(self.z + up, 4)

    def group(self, i):
        return lax.rem(self.y + i, 4)

    def slot(self, up, other, i):
        core = self.c + other * (1 - 2 * self.c)
        return (self.layer(up) * 2 + core) * 4 + self.group(i)

    def in_plane(self, i, j):
        return lax.rem(self.y + i, 4) * 4 + lax.rem(self.x + j, 4)

    def at_layer(self, up):
        return (self.layer(up) * 2 + self.c, self.e)

    def plane_peers(self):
        return [(self.s, lax.rem(self.e + d, 16)) for d in range(1, 16)]

    def column_peers(self):
        return [(lax.rem(self.s + d, 8), self.e) for d in range(1, 8)]


def greet(peers):
    for peer in peers:
        pl.semaphore_signal(
            pltpu.get_barrier_semaphore(), inc=1, device_id=peer, device_id_type=MESH
        )


def greeted(count):
    pl.semaphore_wait(pltpu.get_barrier_semaphore(), count)


def push(src, dst, send_sem, recv_sem, device):
    copy = pltpu.make_async_remote_copy(
        src_ref=src,
        dst_ref=dst,
        send_sem=send_sem,
        recv_sem=recv_sem,
        device_id=device,
        device_id_type=MESH,
    )
    copy.start()
    return copy


def landed(dst, recv_sem, device):
    pltpu.make_async_remote_copy(
        src_ref=dst,
        dst_ref=dst,
        send_sem=recv_sem,
        recv_sem=recv_sem,
        device_id=device,
        device_id_type=MESH,
    ).wait_recv()


HOPS = [(i, j) for i in range(4) for j in (0, 1, 3, 2)]
NT = (((1,), (1,)), ((), ()))
TN = (((0,), (0,)), ((), ()))


def dot(a, b):
    return jnp.dot(a, b, preferred_element_type=F32)


def thirds(v):
    first = v.astype(BF)
    rest = v - first.astype(F32)
    second = rest.astype(BF)
    return first, second, (rest - second.astype(F32)).astype(BF)


def tiles(count, width, body):
    def step(j, carry):
        body(j, pl.ds(pl.multiple_of(j * width, width), width))
        return carry

    lax.fori_loop(0, count, step, 0)


def layer_kernel(
    tok_h, cot_h, wg_h, wu_h, wd_h, router, thr, scale, picks, counts,
    mix_h, tgr_h, gate_h, up_h, down_h, red, thr_out,
    tok, cot, wg, wu, wd, xr, cr, pc, msg, buf, xc, pp, pb, tot, xp, xm, om, rb, ret,
    pre_g, pre_u, hg, hid_t, del_t, wgr, base, mix, tgr, t, ta, tz, tzr, ext, tb,
    s1, r1, sp, rp, sm, rm, sq, rq, es, er, tps, tpr, tms, tmr, s3, r3,
    pas, par, zs, zr, sb, rbs, loc,
):
    at = Spot()
    plane = at.plane_peers()
    column = at.column_peers()
    greet(plane + column)
    loads = [
        pltpu.make_async_copy(a, b, loc.at[k])
        for k, (a, b) in enumerate(
            [(tok_h, tok), (cot_h, cot), (wg_h, wg), (wu_h, wu), (wd_h, wd)]
        )
    ]
    loads[0].start()

    row = lax.broadcasted_iota(jnp.int32, (64, 16), 0)
    lane = lax.broadcasted_iota(jnp.int32, (64, 16), 1)
    mine16 = (lax.div(row, 4) == lane).astype(F32)
    turn = lax.rem(row, 4)
    listed = picks[...].astype(F32)
    wide = jnp.zeros((64, 16), F32)
    for k in range(4):
        wide = jnp.where(turn == k, listed[k : k + 1, :], wide)
    pick = jnp.sum(wide * mine16, axis=1, keepdims=True)
    limit = jnp.sum(mine16 * counts[...].astype(F32), axis=1, keepdims=True)
    live = (turn[:, 0:1].astype(F32) < limit).astype(F32)
    select = (
        pick == lax.broadcasted_iota(jnp.int32, (64, 256), 1).astype(F32)
    ).astype(F32)
    select_bf = select.astype(BF)
    loads[0].wait()
    loads[1].start()

    def take_rows(j, cols):
        xr[:, cols] = dot(select_bf, tok[:, cols]).astype(BF)

    tiles(8, 512, take_rows)
    for e in range(16):
        msg[0, e] = xr[4 * e : 4 * e + 4, :]
    greeted(22)

    sent = []

    def scatter(kind):
        mine = pltpu.make_async_copy(msg.at[kind, at.e], buf.at[kind, at.e], loc.at[5 + kind])
        mine.start()
        for i, j in HOPS:
            if i or j:
                e = at.in_plane(4 - i, j)
                k = i * 4 + j
                sent.append(
                    push(
                        msg.at[kind, e], buf.at[kind, at.e], s1.at[kind, k], r1.at[kind, k],
                        (at.s, e),
                    )
                )
        mine.wait()

    scatter(0)
    gates = jax.nn.sigmoid(
        lax.dot_general(tok[...], router[...], NT, preferred_element_type=F32) - thr[...]
    )
    chosen_gates = jnp.dot(select, gates, precision=HIGH, preferred_element_type=F32)
    raw = jnp.sum(chosen_gates * mine16, axis=1, keepdims=True)
    gate = raw * live
    loads[1].wait()
    for load in loads[2:]:
        load.start()

    def take_cots(j, cols):
        cots = dot(select_bf, cot[:, cols])
        pc[:, cols] = cots.astype(BF)
        cr[:, cols] = (cots * gate).astype(BF)

    tiles(8, 512, take_cots)
    for e in range(16):
        msg[1, e] = cr[4 * e : 4 * e + 4, :]
    scatter(1)

    def hand_over(kind, slot, q):
        ref = xc.at[kind, slot]
        sent.append(push(ref, ref, sq.at[kind, q], rq.at[kind, q], at.partner))

    def climb(kind, slot, k):
        ref = xc.at[kind, slot]
        sent.append(push(ref, ref, sp.at[kind, k], rp.at[kind, k], at.above))

    def sink(kind, slot, k):
        ref = xc.at[kind, slot]
        sent.append(push(ref, ref, sm.at[kind, k], rm.at[kind, k], at.below))

    def gather(kind, i):
        group = at.group(i)
        slot = at.slot(0, 0, i)
        for j in range(4):
            if i or j:
                landed(buf.at[kind, at.in_plane(i, 4 - j)], r1.at[kind, i * 4 + j], at.partner)
        for x in range(4):
            xc[kind, slot, 4 * x : 4 * x + 4, :] = buf[kind, group * 4 + x]
        climb(kind, slot, i)
        sink(kind, slot, i)
        hand_over(kind, slot, i)

    def from_beside(kind, i):
        slot = at.slot(3, 0, i)
        landed(xc.at[kind, slot], rp.at[kind, i], at.above)
        if i in UP:
            climb(kind, slot, 4 + UP.index(i))
        hand_over(kind, slot, 4 + i)
        slot = at.slot(1, 0, i)
        landed(xc.at[kind, slot], rm.at[kind, i], at.below)
        if i in DOWN:
            sink(kind, slot, 4 + DOWN.index(i))
        hand_over(kind, slot, 8 + i)

    def from_across(kind, i):
        slot = at.slot(2, 0, i)
        if i in UP:
            landed(xc.at[kind, slot], rp.at[kind, 4 + UP.index(i)], at.above)
        else:
            landed(xc.at[kind, slot], rm.at[kind, 4 + DOWN.index(i)], at.below)
        hand_over(kind, slot, 12 + i)

    def from_partner(kind, up):
        first = (0, 8, 12, 4)[up]
        for i in range(4):
            landed(xc.at[kind, at.slot(up, 1, i)], rq.at[kind, first + i], at.partner)

    def stacked(kind, lays, cols, width):
        parts = [xc[kind, pl.ds(lay * 8, 8), :, cols].reshape(128, width) for lay in lays]
        return parts[0] if len(parts) == 1 else jnp.concatenate(parts, axis=0)

    def spread(kind, lays, cols, v):
        for n, lay in enumerate(lays):
            piece = v[128 * n : 128 * n + 128]
            pp[kind, pl.ds(lay * 8, 8), :, cols] = piece.astype(BF).reshape(8, 16, 512)

    def keep_t(ref, first, lays, v):
        for n, lay in enumerate(lays):
            cols = pl.ds(pl.multiple_of(lay * 128, 128), 128)
            ref[first : first + 192, cols] = v[128 * n : 128 * n + 128].T.astype(BF)

    def forward(*ups):
        lays = [at.layer(up) for up in ups]
        rows = 128 * len(ups)
        low = {1: 0, 2: 256, 0: 384}[ups[0]]
        span = slice(low, low + rows)
        pre_g[span] = jnp.zeros((rows, 192), F32)
        pre_u[span] = jnp.zeros((rows, 192), F32)

        def before(j, cols):
            a = stacked(0, lays, cols, 1024)
            pre_g[span] += lax.dot_general(a, wg[:, cols], NT, preferred_element_type=F32)
            pre_u[span] += lax.dot_general(a, wu[:, cols], NT, preferred_element_type=F32)

        tiles(4, 1024, before)
        g = pre_g[span]
        hidden = g * jax.nn.sigmoid(g) * pre_u[span] * scale[...]
        h = hidden.astype(BF)
        keep_t(hid_t, 0, lays, hidden)

        def after(j, cols):
            spread(0, lays, cols, dot(h, wd[:, cols]))

        tiles(8, 512, after)

    def backward(*ups):
        lays = [at.layer(up) for up in ups]
        rows = 128 * len(ups)
        low = {1: 0, 2: 256, 0: 384}[ups[0]]
        span = slice(low, low + rows)
        hg[0:rows] = jnp.zeros((rows, 192), F32)

        def before(j, cols):
            a = stacked(1, lays, cols, 1024)
            hg[0:rows] += lax.dot_general(a, wd[:, cols], NT, preferred_element_type=F32)

        tiles(4, 1024, before)
        g = pre_g[span]
        sig = jax.nn.sigmoid(g)
        grad = hg[0:rows] * scale[...]
        gate_delta = grad * pre_u[span] * sig * (1.0 + g * (1.0 - sig))
        up_delta = grad * (g * sig)
        gd = gate_delta.astype(BF)
        ud = up_delta.astype(BF)
        keep_t(del_t, 0, lays, gate_delta)
        keep_t(del_t, 192, lays, up_delta)

        def after(j, cols):
            spread(1, lays, cols, dot(gd, wg[:, cols]) + dot(ud, wu[:, cols]))

        tiles(8, 512, after)

    def trade(kind, up):
        slots = pl.ds(at.slot(up, 1, 0) - at.y, 4)
        sent.append(
            push(pp.at[kind, slots], pb.at[kind, up], es.at[kind, up], er.at[kind, up], at.partner)
        )

    def traded(kind, up):
        landed(pb.at[kind, up], er.at[kind, up], at.partner)

    def combine(kind, up, i, extra):
        q = up * 4 + i
        parts = [pp.at[kind, at.slot(up, 0, i)], pb.at[kind, up, at.group(i)]] + extra

        def add(j, cols):
            acc = parts[0][:, cols].astype(F32)
            for part in parts[1:]:
                acc = acc + part[:, cols].astype(F32)
            tot[kind, q, :, cols] = acc.astype(BF)

        tiles(4, 1024, add)
        return tot.at[kind, q]

    def up_send(kind, src, k):
        sent.append(push(src, xp.at[kind, k], tps.at[kind, k], tpr.at[kind, k], at.above))

    def down_send(kind, src, k):
        sent.append(push(src, xm.at[kind, k], tms.at[kind, k], tmr.at[kind, k], at.below))

    def from_below(kind, k):
        landed(xp.at[kind, k], tpr.at[kind, k], at.above)
        return xp.at[kind, k]

    def from_above(kind, k):
        landed(xm.at[kind, k], tmr.at[kind, k], at.below)
        return xm.at[kind, k]

    def send_plain(kind):
        for k in range(2):
            up_send(kind, combine(kind, 1, DOWN[k], []), k)
            down_send(kind, combine(kind, 3, UP[k], []), k)

    def send_across(kind):
        for k in range(2):
            up_send(kind, combine(kind, 2, UP[k], []), 2 + k)
            down_send(kind, combine(kind, 2, DOWN[k], []), 2 + k)

    def send_merged(kind):
        for k in range(2):
            up_send(kind, combine(kind, 1, UP[k], [from_below(kind, 2 + k)]), 4 + k)
            down_send(kind, combine(kind, 3, DOWN[k], [from_above(kind, 2 + k)]), 4 + k)

    def send_home(kind):
        for i in (1, 0, 3, 2):
            k = i // 2
            if i in UP:
                extra = [from_above(kind, k), from_below(kind, 4 + k)]
            else:
                extra = [from_below(kind, k), from_above(kind, 4 + k)]
            sums = combine(kind, 0, i, extra)
            for x in range(4):
                om[kind, i * 4 + x] = sums[4 * x : 4 * x + 4, :]
            for j in (1, 3, 2, 0):
                e = at.in_plane(i, j)
                src = om.at[kind, i * 4 + lax.rem(at.x + j, 4)]
                k = i * 4 + j
                if k:
                    sent.append(
                        push(src, rb.at[kind, at.e], s3.at[kind, k], r3.at[kind, k], (at.s, e))
                    )
                else:
                    pltpu.make_async_copy(src, rb.at[kind, at.e], loc.at[7 + kind]).start()

    def came_home(kind):
        for i, j in HOPS:
            e = at.in_plane(4 - i, 4 - j)
            if i or j:
                landed(rb.at[kind, e], r3.at[kind, i * 4 + j], at.partner)
            else:
                pltpu.make_async_copy(om.at[kind, at.x], rb.at[kind, e], loc.at[7 + kind]).wait()
        for e in range(16):
            ret[kind, 4 * e : 4 * e + 4, :] = rb[kind, e]

    for i in range(4):
        gather(0, i)
    from_beside(0, 0)
    gather(1, 0)
    gather(1, 1)
    from_beside(0, 1)
    gather(1, 2)
    gather(1, 3)
    from_partner(0, 0)
    for load in loads[2:]:
        load.wait()
    forward(0)
    trade(0, 0)
    from_beside(0, 2)
    from_beside(0, 3)
    from_across(0, 0)
    from_across(0, 1)
    from_partner(0, 3)
    from_partner(0, 1)
    forward(1, 3)
    trade(0, 1)
    trade(0, 3)
    from_beside(1, 0)
    from_beside(1, 1)
    from_across(0, 2)
    from_across(0, 3)
    traded(0, 1)
    traded(0, 3)
    send_plain(0)
    from_partner(0, 2)
    forward(2)
    trade(0, 2)
    from_beside(1, 2)
    from_beside(1, 3)
    from_partner(1, 0)
    traded(0, 2)
    send_across(0)
    from_across(1, 0)
    from_across(1, 1)
    backward(0)
    trade(1, 0)
    from_across(1, 2)
    from_across(1, 3)
    from_partner(1, 3)
    from_partner(1, 1)
    backward(1, 3)
    trade(1, 1)
    trade(1, 3)
    send_merged(0)
    from_partner(1, 2)
    traded(1, 1)
    traded(1, 3)
    send_plain(1)
    backward(2)
    trade(1, 2)
    traded(1, 2)
    send_across(1)

    def weight_tile(j, cols):
        v = dot(del_t[...], xc[0, :, :, cols].reshape(512, 512))
        wgr[0, :, cols] = v[0:192]
        wgr[1, :, cols] = v[192:384]
        c = xc[1, :, :, cols].reshape(512, 512)
        wgr[2, :, cols] = dot(hid_t[...], c)

    tiles(8, 512, weight_tile)
    grads_out = [
        pltpu.make_async_copy(wgr.at[k], ref, loc.at[12 + k])
        for k, ref in enumerate((gate_h, up_h, down_h))
    ]
    for copy in grads_out:
        copy.start()
    traded(0, 0)
    send_home(0)
    came_home(0)

    pulls = jnp.zeros((64, 1), F32)
    for j in range(4):
        cols = slice(1024 * j, 1024 * j + 1024)
        pulls = pulls + jnp.sum(
            pc[:, cols].astype(F32) * ret[0, :, cols].astype(F32), axis=1, keepdims=True
        )
    score = live * pulls * raw * (1.0 - raw)
    by_row = select * score
    sgt = lax.dot_general(mine16, by_row, TN, precision=HIGH, preferred_element_type=F32)
    sg = lax.dot_general(by_row, mine16, TN, precision=HIGH, preferred_element_type=F32)
    parts = jnp.concatenate([v.astype(F32) for v in thirds(sgt)], axis=0).astype(BF)
    bias = jnp.sum(sg, axis=0, keepdims=True)
    bias = jnp.concatenate([bias, jnp.zeros((1, 112), F32)], axis=1)
    bias = jnp.broadcast_to(bias, (16, 128))

    def router_tile(j, cols):
        v = dot(parts, tok[:, cols])
        core, lay = lax.rem(j, 2), lax.div(j, 2)
        t[core, lay, :, 0:512] = v[0:16] + v[16:32] + v[32:48]
        t[core, lay, :, 512:640] = bias

    tiles(8, 512, router_tile)
    sent.append(push(t.at[1 - at.c], ta, pas, par, at.partner))
    send_merged(1)
    landed(ta, par, at.partner)
    tz[...] = t[at.c] + ta[...]
    for d in range(1, 4):
        sent.append(
            push(tz.at[at.layer(d)], tzr.at[d - 1], zs.at[d - 1], zr.at[d - 1], at.at_layer(d))
        )

    w1, w2, w3 = thirds((select * gate).T)
    sg1, sg2, sg3 = thirds(sg)

    def mix_tile(j, cols):
        rows = ret[0, :, cols]
        mix[:, cols] = (dot(w1, rows) + dot(w2, rows) + dot(w3, rows)).astype(BF)
        r = router[:, cols]
        base[:, cols] = dot(sg1, r) + dot(sg2, r) + dot(sg3, r)

    tiles(8, 512, mix_tile)
    mix_out = pltpu.make_async_copy(mix, mix_h, loc.at[10])
    mix_out.start()
    traded(1, 0)
    send_home(1)
    acc = tz[at.z]
    for d in range(3):
        landed(tzr.at[d], zr.at[d], at.partner)
        acc = acc + tzr[d]
    for y in range(4):
        ext[y, :, 0:128] = acc[:, 128 * y : 128 * y + 128]
        ext[y, :, 128:256] = acc[:, 512:640]
    for d, peer in enumerate(plane):
        sent.append(push(ext.at[lax.div(peer[1], 4)], tb.at[d], sb.at[d], rbs.at[d], peer))
    came_home(1)
    select_t = select.T.astype(BF)

    def grad_tile(j, cols):
        tgr[:, cols] = (base[:, cols] + dot(select_t, ret[1, :, cols])).astype(BF)

    tiles(8, 512, grad_tile)
    grad_out = pltpu.make_async_copy(tgr, tgr_h, loc.at[11])
    grad_out.start()
    done = ext[at.y]
    for d in range(15):
        landed(tb.at[d], rbs.at[d], at.partner)
        done = done + tb[d]
    quarter = jnp.zeros((16, 32), F32)
    for x in range(4):
        quarter = jnp.where(at.x == x, done[:, 32 * x : 32 * x + 32], quarter)
    red[...] = quarter
    thr_out[...] = -done[0:1, 128:144]
    for copy in sent:
        copy.wait_send()
    for copy in grads_out:
        copy.wait()
    mix_out.wait()
    grad_out.wait()


def layer(tokens, cotangent, wg, wu, wd, router, thr, scale, picks, counts):
    vmem = pl.BlockSpec(memory_space=pltpu.VMEM)
    hbm = pl.BlockSpec(memory_space=pl.ANY)
    dma = pltpu.SemaphoreType.DMA
    v = pltpu.VMEM
    width = tokens.shape[1]
    units = wg.shape[0]
    shape = jax.ShapeDtypeStruct
    return pl.pallas_call(
        layer_kernel,
        out_shape=(
            shape((256, width), BF),
            shape((256, width), BF),
            shape((units, width), F32),
            shape((units, width), F32),
            shape((units, width), F32),
            shape((16, 32), F32),
            shape((1, 16), F32),
        ),
        in_specs=[hbm] * 5 + [vmem] * 5,
        out_specs=(hbm, hbm, hbm, hbm, hbm, vmem, vmem),
        scratch_shapes=[
            v((256, width), BF), v((256, width), BF),
            v((units, width), BF), v((units, width), BF), v((units, width), BF),
            v((64, width), BF), v((64, width), BF), v((64, width), BF),
            v((2, 16, 4, width), BF), v((2, 16, 4, width), BF),
            v((2, 32, 16, width), BF), v((2, 32, 16, width), BF),
            v((2, 4, 4, 16, width), BF), v((2, 16, 16, width), BF),
            v((2, 6, 16, width), BF), v((2, 6, 16, width), BF),
            v((2, 16, 4, width), BF), v((2, 16, 4, width), BF), v((2, 64, width), BF),
            v((512, units), F32), v((512, units), F32), v((256, units), F32),
            v((units, 512), BF), v((2 * units, 512), BF), v((3, units, width), F32),
            v((256, width), F32), v((256, width), BF), v((256, width), BF),
            v((2, 4, 16, 640), F32), v((4, 16, 640), F32), v((4, 16, 640), F32),
            v((3, 16, 640), F32), v((4, 16, 256), F32), v((15, 16, 256), F32),
            dma((2, 16)), dma((2, 16)), dma((2, 6)), dma((2, 6)), dma((2, 6)), dma((2, 6)),
            dma((2, 16)), dma((2, 16)), dma((2, 4)), dma((2, 4)),
            dma((2, 6)), dma((2, 6)), dma((2, 6)), dma((2, 6)),
            dma((2, 16)), dma((2, 16)), dma, dma, dma((3,)), dma((3,)),
            dma((15,)), dma((15,)), dma((15,)),
        ],
        compiler_params=pltpu.CompilerParams(
            collective_id=0, has_side_effects=True, vmem_limit_bytes=67043328
        ),
    )(tokens, cotangent, wg, wu, wd, router, thr, scale, picks, counts)


def on_device(tokens, cotangent, router, threshold, w_gate, w_up, w_down, hid_scale, picks, counts):
    mixture, token_grad, gate_grad, up_grad, down_grad, reduced, thresholds = layer(
        tokens, cotangent, w_gate[0].T, w_up[0].T, w_down[0], router.T,
        threshold[None, :], hid_scale, picks[0].T, counts,
    )
    return (
        mixture,
        token_grad,
        reduced.T,
        thresholds[0],
        gate_grad.T[None],
        up_grad.T[None],
        down_grad[None],
    )


def solution(mesh):
    placed = (
        P(("seq", "exp"), None),
        P(("seq", "exp"), None),
        P(),
        P(),
        P("exp", None, "seq"),
        P("exp", None, "seq"),
        P("exp", "seq", None),
        P("exp", "seq"),
        P(("seq", "exp"), None, None),
        P(("seq", "exp"), None),
    )
    return jax.shard_map(
        on_device,
        mesh=mesh,
        in_specs=placed,
        out_specs=(
            P(("seq", "exp"), None),
            P(("seq", "exp"), None),
            P(("seq", "exp"), None),
            P(),
            P("exp", None, "seq"),
            P("exp", None, "seq"),
            P("exp", "seq", None),
        ),
        check_vma=False,
    )
```

```python
import jax
import jax.numpy as jnp
from jax import lax
from jax.experimental import pallas as pl
from jax.experimental.pallas import tpu as pltpu
from jax.sharding import PartitionSpec as P

MESH = pl.DeviceIdType.MESH
BF = jnp.bfloat16
F32 = jnp.float32
HIGH = lax.Precision.HIGHEST
UP = (2, 0)
DOWN = (1, 3)


class Spot:
    def __init__(self):
        self.s = lax.axis_index("seq")
        self.e = lax.axis_index("exp")
        self.z = lax.div(self.s, 2)
        self.c = lax.rem(self.s, 2)
        self.y = lax.div(self.e, 4)
        self.x = lax.rem(self.e, 4)
        self.partner = (self.s + 1 - 2 * self.c, self.e)
        self.above = (self.layer(1) * 2 + self.c, self.e)
        self.below = (self.layer(3) * 2 + self.c, self.e)

    def layer(self, up):
        return lax.rem(self.z + up, 4)

    def group(self, i):
        return lax.rem(self.y + i, 4)

    def slot(self, up, other, i):
        core = self.c + other * (1 - 2 * self.c)
        return (self.layer(up) * 2 + core) * 4 + self.group(i)

    def in_plane(self, i, j):
        return lax.rem(self.y + i, 4) * 4 + lax.rem(self.x + j, 4)

    def at_layer(self, up):
        return (self.layer(up) * 2 + self.c, self.e)

    def plane_peers(self):
        return [(self.s, lax.rem(self.e + d, 16)) for d in range(1, 16)]

    def column_peers(self):
        return [(lax.rem(self.s + d, 8), self.e) for d in range(1, 8)]


def greet(peers):
    for peer in peers:
        pl.semaphore_signal(
            pltpu.get_barrier_semaphore(), inc=1, device_id=peer, device_id_type=MESH
        )


def greeted(count):
    pl.semaphore_wait(pltpu.get_barrier_semaphore(), count)


def push(src, dst, send_sem, recv_sem, device):
    copy = pltpu.make_async_remote_copy(
        src_ref=src,
        dst_ref=dst,
        send_sem=send_sem,
        recv_sem=recv_sem,
        device_id=device,
        device_id_type=MESH,
    )
    copy.start()
    return copy


def landed(dst, recv_sem, device):
    pltpu.make_async_remote_copy(
        src_ref=dst,
        dst_ref=dst,
        send_sem=recv_sem,
        recv_sem=recv_sem,
        device_id=device,
        device_id_type=MESH,
    ).wait_recv()


HOPS = [(i, j) for i in range(4) for j in (0, 1, 3, 2)]
NT = (((1,), (1,)), ((), ()))
TN = (((0,), (0,)), ((), ()))


def dot(a, b):
    return jnp.dot(a, b, preferred_element_type=F32)


def thirds(v):
    first = v.astype(BF)
    rest = v - first.astype(F32)
    second = rest.astype(BF)
    return first, second, (rest - second.astype(F32)).astype(BF)


def tiles(count, width, body):
    def step(j, carry):
        body(j, pl.ds(pl.multiple_of(j * width, width), width))
        return carry

    lax.fori_loop(0, count, step, 0)


def joined(pieces, axis):
    return jnp.concatenate([v.astype(F32) for v in pieces], axis=axis).astype(BF)


def layer_kernel(
    tok_h, cot_h, wg_h, wu_h, wd_h, router, thr, scale, picks, counts,
    mix, tgr, gate_w, up_w, down_w, red, thr_out,
    tok, cot, wg, wu, wd, xr, cr, pc, msg, buf, xc, pp, pb, xp, xm, om, rb, ret,
    pre_g, pre_u, hg, hid_t, del_t, base, t, ta, tz, tzr, ext, tb,
    s1, r1, sp, rp, sm, rm, sq, rq, es, er, tps, tpr, tms, tmr, s3, r3,
    pas, par, zs, zr, sb, rbs, loc,
):
    at = Spot()
    plane = at.plane_peers()
    column = at.column_peers()
    greet(plane + column)
    loads = [
        pltpu.make_async_copy(a, b, loc.at[k])
        for k, (a, b) in enumerate([(cot_h, cot), (wg_h, wg), (wu_h, wu), (wd_h, wd)])
    ]
    pieces = []
    for k in range(4):
        cols = slice(1024 * k, 1024 * k + 1024)
        pieces.append(pltpu.make_async_copy(tok_h.at[:, cols], tok.at[:, cols], loc.at[9 + k]))
        pieces[k].start()

    row = lax.broadcasted_iota(jnp.int32, (64, 16), 0)
    lane = lax.broadcasted_iota(jnp.int32, (64, 16), 1)
    mine16 = (lax.div(row, 4) == lane).astype(F32)
    turn = lax.rem(row, 4)
    listed = picks[...].astype(F32)
    wide = jnp.zeros((64, 16), F32)
    for k in range(4):
        wide = jnp.where(turn == k, listed[k : k + 1, :], wide)
    pick = jnp.sum(wide * mine16, axis=1, keepdims=True)
    limit = jnp.sum(mine16 * counts[...].astype(F32), axis=1, keepdims=True)
    live = (turn[:, 0:1].astype(F32) < limit).astype(F32)
    select = (
        pick == lax.broadcasted_iota(jnp.int32, (64, 256), 1).astype(F32)
    ).astype(F32)
    select_bf = select.astype(BF)
    loads[0].start()

    for k in range(4):
        cols = slice(1024 * k, 1024 * k + 1024)
        pieces[k].wait()
        xr[:, cols] = dot(select_bf, tok[:, cols]).astype(BF)
    for e in range(16):
        msg[0, e] = xr[4 * e : 4 * e + 4, :]
    greeted(22)

    sent = []

    def scatter(kind):
        mine = pltpu.make_async_copy(msg.at[kind, at.e], buf.at[kind, at.e], loc.at[5 + kind])
        mine.start()
        for i, j in HOPS:
            if i or j:
                e = at.in_plane(4 - i, j)
                k = i * 4 + j
                sent.append(
                    push(
                        msg.at[kind, e], buf.at[kind, at.e], s1.at[kind, k], r1.at[kind, k],
                        (at.s, e),
                    )
                )
        mine.wait()

    scatter(0)
    gates = jax.nn.sigmoid(
        lax.dot_general(tok[...], router[...], NT, preferred_element_type=F32) - thr[...]
    )
    chosen_gates = jnp.dot(select, gates, precision=HIGH, preferred_element_type=F32)
    raw = jnp.sum(chosen_gates * mine16, axis=1, keepdims=True)
    gate = raw * live
    loads[0].wait()
    for load in loads[1:]:
        load.start()

    def take_cots(j, cols):
        cots = dot(select_bf, cot[:, cols])
        pc[:, cols] = cots.astype(BF)
        cr[:, cols] = (cots * gate).astype(BF)

    tiles(8, 512, take_cots)
    for e in range(16):
        msg[1, e] = cr[4 * e : 4 * e + 4, :]
    scatter(1)

    def hand_over(kind, slot, q):
        ref = xc.at[kind, slot]
        sent.append(push(ref, ref, sq.at[kind, q], rq.at[kind, q], at.partner))

    def climb(kind, slot, k):
        ref = xc.at[kind, slot]
        sent.append(push(ref, ref, sp.at[kind, k], rp.at[kind, k], at.above))

    def sink(kind, slot, k):
        ref = xc.at[kind, slot]
        sent.append(push(ref, ref, sm.at[kind, k], rm.at[kind, k], at.below))

    def gather(kind, i):
        group = at.group(i)
        slot = at.slot(0, 0, i)
        for j in range(4):
            if i or j:
                landed(buf.at[kind, at.in_plane(i, 4 - j)], r1.at[kind, i * 4 + j], at.partner)
        for x in range(4):
            xc[kind, slot, 4 * x : 4 * x + 4, :] = buf[kind, group * 4 + x]
        climb(kind, slot, i)
        sink(kind, slot, i)
        hand_over(kind, slot, i)

    def from_beside(kind, i):
        slot = at.slot(3, 0, i)
        landed(xc.at[kind, slot], rp.at[kind, i], at.above)
        if i in UP:
            climb(kind, slot, 4 + UP.index(i))
        hand_over(kind, slot, 4 + i)
        slot = at.slot(1, 0, i)
        landed(xc.at[kind, slot], rm.at[kind, i], at.below)
        if i in DOWN:
            sink(kind, slot, 4 + DOWN.index(i))
        hand_over(kind, slot, 8 + i)

    def from_across(kind, i):
        slot = at.slot(2, 0, i)
        if i in UP:
            landed(xc.at[kind, slot], rp.at[kind, 4 + UP.index(i)], at.above)
        else:
            landed(xc.at[kind, slot], rm.at[kind, 4 + DOWN.index(i)], at.below)
        hand_over(kind, slot, 12 + i)

    def from_partner(kind, up):
        first = (0, 8, 12, 4)[up]
        for i in range(4):
            landed(xc.at[kind, at.slot(up, 1, i)], rq.at[kind, first + i], at.partner)

    def stacked(kind, lays, cols, width):
        parts = [xc[kind, pl.ds(lay * 8, 8), :, cols].reshape(128, width) for lay in lays]
        return parts[0] if len(parts) == 1 else jnp.concatenate(parts, axis=0)

    def spread(kind, lays, cols, v):
        for n, lay in enumerate(lays):
            piece = v[128 * n : 128 * n + 128]
            pp[kind, pl.ds(lay * 8, 8), :, cols] = piece.astype(BF).reshape(8, 16, 512)

    def keep_t(ref, first, lays, v):
        for n, lay in enumerate(lays):
            cols = pl.ds(pl.multiple_of(lay * 128, 128), 128)
            ref[first : first + 192, cols] = v[128 * n : 128 * n + 128].T.astype(BF)

    def forward(*ups):
        lays = [at.layer(up) for up in ups]
        rows = 128 * len(ups)
        low = {1: 0, 2: 256, 0: 384}[ups[0]]
        span = slice(low, low + rows)
        pre_g[span] = jnp.zeros((rows, 192), F32)
        pre_u[span] = jnp.zeros((rows, 192), F32)

        def before(j, cols):
            a = stacked(0, lays, cols, 1024)
            pre_g[span] += lax.dot_general(a, wg[:, cols], NT, preferred_element_type=F32)
            pre_u[span] += lax.dot_general(a, wu[:, cols], NT, preferred_element_type=F32)

        tiles(4, 1024, before)
        g = pre_g[span]
        hidden = g * jax.nn.sigmoid(g) * pre_u[span] * scale[...]
        h = hidden.astype(BF)
        keep_t(hid_t, 0, lays, hidden)

        def after(j, cols):
            spread(0, lays, cols, dot(h, wd[:, cols]))

        tiles(8, 512, after)

    def backward(*ups):
        lays = [at.layer(up) for up in ups]
        rows = 128 * len(ups)
        low = {1: 0, 2: 256, 0: 384}[ups[0]]
        span = slice(low, low + rows)
        hg[0:rows] = jnp.zeros((rows, 192), F32)

        def before(j, cols):
            a = stacked(1, lays, cols, 1024)
            hg[0:rows] += lax.dot_general(a, wd[:, cols], NT, preferred_element_type=F32)

        tiles(4, 1024, before)
        g = pre_g[span]
        sig = jax.nn.sigmoid(g)
        grad = hg[0:rows] * scale[...]
        gate_delta = grad * pre_u[span] * sig * (1.0 + g * (1.0 - sig))
        up_delta = grad * (g * sig)
        gd = gate_delta.astype(BF)
        ud = up_delta.astype(BF)
        keep_t(del_t, 0, lays, gate_delta)
        keep_t(del_t, 192, lays, up_delta)

        def after(j, cols):
            spread(1, lays, cols, dot(gd, wg[:, cols]) + dot(ud, wu[:, cols]))

        tiles(8, 512, after)

    def trade(kind, up):
        slots = pl.ds(at.slot(up, 1, 0) - at.y, 4)
        sent.append(
            push(pp.at[kind, slots], pb.at[kind, up], es.at[kind, up], er.at[kind, up], at.partner)
        )

    def traded(kind, up):
        landed(pb.at[kind, up], er.at[kind, up], at.partner)

    def combine(kind, up, i, extra):
        parts = [pp.at[kind, at.slot(up, 0, i)], pb.at[kind, up, at.group(i)]] + extra

        def add(j, cols):
            acc = parts[0][:, cols].astype(F32)
            for part in parts[1:]:
                acc = acc + part[:, cols].astype(F32)
            parts[1][:, cols] = acc.astype(BF)

        tiles(4, 1024, add)
        return parts[1]

    def up_send(kind, src, k):
        sent.append(push(src, xp.at[kind, k], tps.at[kind, k], tpr.at[kind, k], at.above))

    def down_send(kind, src, k):
        sent.append(push(src, xm.at[kind, k], tms.at[kind, k], tmr.at[kind, k], at.below))

    def from_below(kind, k):
        landed(xp.at[kind, k], tpr.at[kind, k], at.above)
        return xp.at[kind, k]

    def from_above(kind, k):
        landed(xm.at[kind, k], tmr.at[kind, k], at.below)
        return xm.at[kind, k]

    def send_plain(kind):
        for k in range(2):
            up_send(kind, combine(kind, 1, DOWN[k], []), k)
            down_send(kind, combine(kind, 3, UP[k], []), k)

    def send_across(kind):
        for k in range(2):
            up_send(kind, combine(kind, 2, UP[k], []), 2 + k)
            down_send(kind, combine(kind, 2, DOWN[k], []), 2 + k)

    def send_merged(kind):
        for k in range(2):
            up_send(kind, combine(kind, 1, UP[k], [from_below(kind, 2 + k)]), 4 + k)
            down_send(kind, combine(kind, 3, DOWN[k], [from_above(kind, 2 + k)]), 4 + k)

    def send_home(kind):
        for i in (DOWN[0], UP[0], DOWN[1], UP[1]):
            if i in UP:
                k = UP.index(i)
                extra = [from_above(kind, k), from_below(kind, 4 + k)]
            else:
                k = DOWN.index(i)
                extra = [from_below(kind, k), from_above(kind, 4 + k)]
            sums = combine(kind, 0, i, extra)
            for x in range(4):
                om[kind, i * 4 + x] = sums[4 * x : 4 * x + 4, :]
            for j in (1, 3, 2, 0):
                e = at.in_plane(i, j)
                src = om.at[kind, i * 4 + lax.rem(at.x + j, 4)]
                k = i * 4 + j
                if k:
                    sent.append(
                        push(src, rb.at[kind, at.e], s3.at[kind, k], r3.at[kind, k], (at.s, e))
                    )
                else:
                    pltpu.make_async_copy(src, rb.at[kind, at.e], loc.at[7 + kind]).start()

    def came_home(kind):
        for i, j in HOPS:
            e = at.in_plane(4 - i, 4 - j)
            if i or j:
                landed(rb.at[kind, e], r3.at[kind, i * 4 + j], at.partner)
            else:
                pltpu.make_async_copy(om.at[kind, at.x], rb.at[kind, e], loc.at[7 + kind]).wait()
        for e in range(16):
            ret[kind, 4 * e : 4 * e + 4, :] = rb[kind, e]

    for i in range(4):
        gather(0, i)
    from_beside(0, 0)
    gather(1, 0)
    gather(1, 1)
    from_beside(0, 1)
    gather(1, 2)
    gather(1, 3)
    from_partner(0, 0)
    for load in loads[1:]:
        load.wait()
    forward(0)
    trade(0, 0)
    from_beside(0, 2)
    from_beside(0, 3)
    from_partner(0, 3)
    from_partner(0, 1)
    forward(1, 3)
    trade(0, 1)
    trade(0, 3)
    from_across(0, 0)
    from_across(0, 1)
    from_beside(1, 0)
    from_beside(1, 1)
    traded(0, 1)
    traded(0, 3)
    send_plain(0)
    from_partner(1, 0)
    backward(0)
    trade(1, 0)
    from_beside(1, 2)
    from_beside(1, 3)
    from_across(0, 2)
    from_across(0, 3)
    from_partner(0, 2)
    forward(2)
    trade(0, 2)
    from_across(1, 0)
    from_across(1, 1)
    traded(0, 2)
    send_across(0)
    from_partner(1, 3)
    from_partner(1, 1)
    backward(1, 3)
    trade(1, 1)
    trade(1, 3)
    from_across(1, 2)
    from_across(1, 3)
    send_merged(0)
    traded(1, 1)
    traded(1, 3)
    send_plain(1)
    from_partner(1, 2)
    backward(2)
    trade(1, 2)
    traded(1, 2)
    send_across(1)

    def weight_tile(j, cols):
        v = dot(del_t[...], xc[0, :, :, cols].reshape(512, 512))
        gate_w[:, cols] = v[0:192]
        up_w[:, cols] = v[192:384]
        c = xc[1, :, :, cols].reshape(512, 512)
        down_w[:, cols] = dot(hid_t[...], c)

    tiles(8, 512, weight_tile)
    traded(0, 0)
    send_home(0)
    send_merged(1)
    came_home(0)

    pulls = jnp.zeros((64, 1), F32)
    for j in range(4):
        cols = slice(1024 * j, 1024 * j + 1024)
        pulls = pulls + jnp.sum(
            pc[:, cols].astype(F32) * ret[0, :, cols].astype(F32), axis=1, keepdims=True
        )
    score = live * pulls * raw * (1.0 - raw)
    by_row = select * score
    sgt = lax.dot_general(mine16, by_row, TN, precision=HIGH, preferred_element_type=F32)
    sg = lax.dot_general(by_row, mine16, TN, precision=HIGH, preferred_element_type=F32)
    parts = joined(thirds(sgt), 0)
    bias = jnp.sum(sg, axis=0, keepdims=True)
    bias = jnp.concatenate([bias, jnp.zeros((1, 112), F32)], axis=1)
    bias = jnp.broadcast_to(bias, (16, 128))

    def router_tile(j, cols):
        v = dot(parts, tok[:, cols])
        core, lay = lax.rem(j, 2), lax.div(j, 2)
        t[core, lay, :, 0:512] = v[0:16] + v[16:32] + v[32:48]
        t[core, lay, :, 512:640] = bias

    tiles(8, 512, router_tile)
    sent.append(push(t.at[1 - at.c], ta, pas, par, at.partner))
    traded(1, 0)
    send_home(1)
    landed(ta, par, at.partner)
    tz[...] = t[at.c] + ta[...]
    for d in range(1, 4):
        sent.append(
            push(tz.at[at.layer(d)], tzr.at[d - 1], zs.at[d - 1], zr.at[d - 1], at.at_layer(d))
        )
    mix_w = joined(thirds((select * gate).T), 1)
    sg_w = joined(thirds(sg), 1)

    def mix_tile(j, cols):
        rows = ret[0, :, cols]
        mix[:, cols] = dot(mix_w, jnp.concatenate([rows] * 3, axis=0)).astype(BF)

    tiles(8, 512, mix_tile)
    acc = tz[at.z]
    for d in range(3):
        landed(tzr.at[d], zr.at[d], at.partner)
        acc = acc + tzr[d]
    for y in range(4):
        ext[y, :, 0:128] = acc[:, 128 * y : 128 * y + 128]
        ext[y, :, 128:256] = acc[:, 512:640]
    for d, peer in enumerate(plane):
        sent.append(push(ext.at[lax.div(peer[1], 4)], tb.at[d], sb.at[d], rbs.at[d], peer))

    def base_tile(j, cols):
        r = router[:, cols]
        base[:, cols] = dot(sg_w, jnp.concatenate([r] * 3, axis=0))

    tiles(8, 512, base_tile)
    for copy in sent:
        copy.wait_send()
    came_home(1)
    select_t = select.T.astype(BF)

    def grad_tile(j, cols):
        tgr[:, cols] = (base[:, cols] + dot(select_t, ret[1, :, cols])).astype(BF)

    tiles(8, 512, grad_tile)
    done = ext[at.y]
    for d in range(15):
        landed(tb.at[d], rbs.at[d], at.partner)
        done = done + tb[d]
    quarter = jnp.zeros((16, 32), F32)
    for x in range(4):
        quarter = jnp.where(at.x == x, done[:, 32 * x : 32 * x + 32], quarter)
    red[...] = quarter
    thr_out[...] = -done[0:1, 128:144]


def layer(tokens, cotangent, wg, wu, wd, router, thr, scale, picks, counts):
    vmem = pl.BlockSpec(memory_space=pltpu.VMEM)
    hbm = pl.BlockSpec(memory_space=pl.ANY)
    dma = pltpu.SemaphoreType.DMA
    v = pltpu.VMEM
    width = tokens.shape[1]
    units = wg.shape[0]
    return pl.pallas_call(
        layer_kernel,
        out_shape=(
            v((256, width), BF),
            v((256, width), BF),
            v((units, width), F32),
            v((units, width), F32),
            v((units, width), F32),
            v((16, 32), F32),
            v((1, 16), F32),
        ),
        in_specs=[hbm] * 5 + [vmem] * 5,
        out_specs=(vmem,) * 7,
        scratch_shapes=[
            v((256, width), BF), v((256, width), BF),
            v((units, width), BF), v((units, width), BF), v((units, width), BF),
            v((64, width), BF), v((64, width), BF), v((64, width), BF),
            v((2, 16, 4, width), BF), v((2, 16, 4, width), BF),
            v((2, 32, 16, width), BF), v((2, 32, 16, width), BF),
            v((2, 4, 4, 16, width), BF),
            v((2, 6, 16, width), BF), v((2, 6, 16, width), BF),
            v((2, 16, 4, width), BF), v((2, 16, 4, width), BF), v((2, 64, width), BF),
            v((512, units), F32), v((512, units), F32), v((256, units), F32),
            v((units, 512), BF), v((2 * units, 512), BF),
            v((256, width), F32),
            v((2, 4, 16, 640), F32), v((4, 16, 640), F32), v((4, 16, 640), F32),
            v((3, 16, 640), F32), v((4, 16, 256), F32), v((15, 16, 256), F32),
            dma((2, 16)), dma((2, 16)), dma((2, 6)), dma((2, 6)), dma((2, 6)), dma((2, 6)),
            dma((2, 16)), dma((2, 16)), dma((2, 4)), dma((2, 4)),
            dma((2, 6)), dma((2, 6)), dma((2, 6)), dma((2, 6)),
            dma((2, 16)), dma((2, 16)), dma, dma, dma((3,)), dma((3,)),
            dma((15,)), dma((15,)), dma((13,)),
        ],
        compiler_params=pltpu.CompilerParams(
            collective_id=0, has_side_effects=True, vmem_limit_bytes=49 << 20
        ),
    )(tokens, cotangent, wg, wu, wd, router, thr, scale, picks, counts)


def on_device(tokens, cotangent, router, threshold, w_gate, w_up, w_down, hid_scale, picks, counts):
    mixture, token_grad, gate_grad, up_grad, down_grad, reduced, thresholds = layer(
        tokens, cotangent, w_gate[0].T, w_up[0].T, w_down[0], router.T,
        threshold[None, :], hid_scale, picks[0].T, counts,
    )
    return (
        mixture,
        token_grad,
        reduced.T,
        thresholds[0],
        gate_grad.T[None],
        up_grad.T[None],
        down_grad[None],
    )


def solution(mesh):
    placed = (
        P(("seq", "exp"), None),
        P(("seq", "exp"), None),
        P(),
        P(),
        P("exp", None, "seq"),
        P("exp", None, "seq"),
        P("exp", "seq", None),
        P("exp", "seq"),
        P(("seq", "exp"), None, None),
        P(("seq", "exp"), None),
    )
    return jax.shard_map(
        on_device,
        mesh=mesh,
        in_specs=placed,
        out_specs=(
            P(("seq", "exp"), None),
            P(("seq", "exp"), None),
            P(("seq", "exp"), None),
            P(),
            P("exp", None, "seq"),
            P("exp", None, "seq"),
            P("exp", "seq", None),
        ),
        check_vma=False,
    )
```

```python
import jax
import jax.numpy as jnp
from jax import lax
from jax.experimental import pallas as pl
from jax.experimental.pallas import tpu as pltpu
from jax.sharding import PartitionSpec as P

MESH = pl.DeviceIdType.MESH
BF = jnp.bfloat16
F32 = jnp.float32
HIGH = lax.Precision.HIGHEST
UP = (2, 0)
DOWN = (1, 3)


class Spot:
    def __init__(self):
        self.s = lax.axis_index("seq")
        self.e = lax.axis_index("exp")
        self.z = lax.div(self.s, 2)
        self.c = lax.rem(self.s, 2)
        self.y = lax.div(self.e, 4)
        self.x = lax.rem(self.e, 4)
        self.partner = (self.s + 1 - 2 * self.c, self.e)
        self.above = (self.layer(1) * 2 + self.c, self.e)
        self.below = (self.layer(3) * 2 + self.c, self.e)

    def layer(self, up):
        return lax.rem(self.z + up, 4)

    def group(self, i):
        return lax.rem(self.y + i, 4)

    def slot(self, up, other, i):
        core = self.c + other * (1 - 2 * self.c)
        return (self.layer(up) * 2 + core) * 4 + self.group(i)

    def in_plane(self, i, j):
        return lax.rem(self.y + i, 4) * 4 + lax.rem(self.x + j, 4)

    def at_layer(self, up):
        return (self.layer(up) * 2 + self.c, self.e)

    def plane_peers(self):
        return [(self.s, lax.rem(self.e + d, 16)) for d in range(1, 16)]

    def column_peers(self):
        return [(lax.rem(self.s + d, 8), self.e) for d in range(1, 8)]


def greet(peers):
    for peer in peers:
        pl.semaphore_signal(
            pltpu.get_barrier_semaphore(), inc=1, device_id=peer, device_id_type=MESH
        )


def greeted(count):
    pl.semaphore_wait(pltpu.get_barrier_semaphore(), count)


def push(src, dst, send_sem, recv_sem, device):
    copy = pltpu.make_async_remote_copy(
        src_ref=src,
        dst_ref=dst,
        send_sem=send_sem,
        recv_sem=recv_sem,
        device_id=device,
        device_id_type=MESH,
    )
    copy.start()
    return copy


def landed(dst, recv_sem, device):
    pltpu.make_async_remote_copy(
        src_ref=dst,
        dst_ref=dst,
        send_sem=recv_sem,
        recv_sem=recv_sem,
        device_id=device,
        device_id_type=MESH,
    ).wait_recv()


HOPS = [(i, j) for i in range(4) for j in (0, 1, 3, 2)]
NT = (((1,), (1,)), ((), ()))
TN = (((0,), (0,)), ((), ()))


def dot(a, b):
    return jnp.dot(a, b, preferred_element_type=F32)


def thirds(v):
    first = v.astype(BF)
    rest = v - first.astype(F32)
    second = rest.astype(BF)
    return first, second, (rest - second.astype(F32)).astype(BF)


def tiles(count, width, body):
    def step(j, carry):
        body(j, pl.ds(pl.multiple_of(j * width, width), width))
        return carry

    lax.fori_loop(0, count, step, 0)


def joined(pieces, axis):
    return jnp.concatenate([v.astype(F32) for v in pieces], axis=axis).astype(BF)


def layer_kernel(
    tok_h, cot_h, wg_h, wu_h, wd_h, router, thr, scale, picks, counts,
    mix, tgr, gate_w, up_w, down_w, red, thr_out,
    tok, cot, wg, wu, wd, xr, cr, pc, msg, buf, xc, pp, pb, xp, xm, om, rb, ret,
    pre_g, pre_u, hg, hid_t, del_t, base, t, ta, tz, tzr, ext, tb,
    s1, r1, sp, rp, sm, rm, sq, rq, es, er, tps, tpr, tms, tmr, s3, r3,
    pas, par, zs, zr, sb, rbs, loc,
):
    at = Spot()
    plane = at.plane_peers()
    column = at.column_peers()
    greet(plane + column)
    loads = [
        pltpu.make_async_copy(a, b, loc.at[k])
        for k, (a, b) in enumerate([(cot_h, cot), (wg_h, wg), (wu_h, wu), (wd_h, wd)])
    ]
    pieces = []
    for k in range(4):
        cols = slice(1024 * k, 1024 * k + 1024)
        pieces.append(pltpu.make_async_copy(tok_h.at[:, cols], tok.at[:, cols], loc.at[9 + k]))
        pieces[k].start()

    row = lax.broadcasted_iota(jnp.int32, (64, 16), 0)
    lane = lax.broadcasted_iota(jnp.int32, (64, 16), 1)
    mine16 = (lax.div(row, 4) == lane).astype(F32)
    turn = lax.rem(row, 4)
    listed = picks[...].astype(F32)
    wide = jnp.zeros((64, 16), F32)
    for k in range(4):
        wide = jnp.where(turn == k, listed[k : k + 1, :], wide)
    pick = jnp.sum(wide * mine16, axis=1, keepdims=True)
    limit = jnp.sum(mine16 * counts[...].astype(F32), axis=1, keepdims=True)
    live = (turn[:, 0:1].astype(F32) < limit).astype(F32)
    select = (
        pick == lax.broadcasted_iota(jnp.int32, (64, 256), 1).astype(F32)
    ).astype(F32)
    select_bf = select.astype(BF)
    loads[0].start()

    for k in range(4):
        cols = slice(1024 * k, 1024 * k + 1024)
        pieces[k].wait()
        xr[:, cols] = dot(select_bf, tok[:, cols]).astype(BF)
    for e in range(16):
        msg[0, e] = xr[4 * e : 4 * e + 4, :]
    greeted(22)

    sent = []

    def scatter(kind):
        mine = pltpu.make_async_copy(msg.at[kind, at.e], buf.at[kind, at.e], loc.at[5 + kind])
        mine.start()
        for i, j in HOPS:
            if i or j:
                e = at.in_plane(4 - i, j)
                k = i * 4 + j
                sent.append(
                    push(
                        msg.at[kind, e], buf.at[kind, at.e], s1.at[kind, k], r1.at[kind, k],
                        (at.s, e),
                    )
                )
        mine.wait()

    scatter(0)
    gates = jax.nn.sigmoid(
        lax.dot_general(tok[...], router[...], NT, preferred_element_type=F32) - thr[...]
    )
    chosen_gates = jnp.dot(select, gates, precision=HIGH, preferred_element_type=F32)
    raw = jnp.sum(chosen_gates * mine16, axis=1, keepdims=True)
    gate = raw * live
    loads[0].wait()
    for load in loads[1:]:
        load.start()

    def take_cots(j, cols):
        cots = dot(select_bf, cot[:, cols])
        pc[:, cols] = cots.astype(BF)
        cr[:, cols] = (cots * gate).astype(BF)

    tiles(8, 512, take_cots)
    for e in range(16):
        msg[1, e] = cr[4 * e : 4 * e + 4, :]
    scatter(1)

    def hand_over(kind, slot, q):
        ref = xc.at[kind, slot]
        sent.append(push(ref, ref, sq.at[kind, q], rq.at[kind, q], at.partner))

    def climb(kind, slot, k):
        ref = xc.at[kind, slot]
        sent.append(push(ref, ref, sp.at[kind, k], rp.at[kind, k], at.above))

    def sink(kind, slot, k):
        ref = xc.at[kind, slot]
        sent.append(push(ref, ref, sm.at[kind, k], rm.at[kind, k], at.below))

    def gather(kind, i):
        group = at.group(i)
        slot = at.slot(0, 0, i)
        for j in range(4):
            if i or j:
                landed(buf.at[kind, at.in_plane(i, 4 - j)], r1.at[kind, i * 4 + j], at.partner)
        for x in range(4):
            xc[kind, slot, 4 * x : 4 * x + 4, :] = buf[kind, group * 4 + x]
        climb(kind, slot, i)
        sink(kind, slot, i)
        hand_over(kind, slot, i)

    def from_beside(kind, i):
        slot = at.slot(3, 0, i)
        landed(xc.at[kind, slot], rp.at[kind, i], at.above)
        if i in UP:
            climb(kind, slot, 4 + UP.index(i))
        hand_over(kind, slot, 4 + i)
        slot = at.slot(1, 0, i)
        landed(xc.at[kind, slot], rm.at[kind, i], at.below)
        if i in DOWN:
            sink(kind, slot, 4 + DOWN.index(i))
        hand_over(kind, slot, 8 + i)

    def from_across(kind, i):
        slot = at.slot(2, 0, i)
        if i in UP:
            landed(xc.at[kind, slot], rp.at[kind, 4 + UP.index(i)], at.above)
        else:
            landed(xc.at[kind, slot], rm.at[kind, 4 + DOWN.index(i)], at.below)
        hand_over(kind, slot, 12 + i)

    def from_partner(kind, up):
        first = (0, 8, 12, 4)[up]
        for i in range(4):
            landed(xc.at[kind, at.slot(up, 1, i)], rq.at[kind, first + i], at.partner)

    def stacked(kind, lays, cols, width):
        parts = [xc[kind, pl.ds(lay * 8, 8), :, cols].reshape(128, width) for lay in lays]
        return parts[0] if len(parts) == 1 else jnp.concatenate(parts, axis=0)

    def spread(kind, lays, cols, v):
        for n, lay in enumerate(lays):
            piece = v[128 * n : 128 * n + 128]
            pp[kind, pl.ds(lay * 8, 8), :, cols] = piece.astype(BF).reshape(8, 16, 512)

    def keep_t(ref, first, lays, v):
        for n, lay in enumerate(lays):
            cols = pl.ds(pl.multiple_of(lay * 128, 128), 128)
            ref[first : first + 192, cols] = v[128 * n : 128 * n + 128].T.astype(BF)

    def forward(*ups):
        lays = [at.layer(up) for up in ups]
        rows = 128 * len(ups)
        low = {1: 0, 2: 256, 0: 384}[ups[0]]
        span = slice(low, low + rows)
        pre_g[span] = jnp.zeros((rows, 192), F32)
        pre_u[span] = jnp.zeros((rows, 192), F32)

        def before(j, cols):
            a = stacked(0, lays, cols, 1024)
            pre_g[span] += lax.dot_general(a, wg[:, cols], NT, preferred_element_type=F32)
            pre_u[span] += lax.dot_general(a, wu[:, cols], NT, preferred_element_type=F32)

        tiles(4, 1024, before)
        g = pre_g[span]
        hidden = g * jax.nn.sigmoid(g) * pre_u[span] * scale[...]
        h = hidden.astype(BF)
        keep_t(hid_t, 0, lays, hidden)

        def after(j, cols):
            spread(0, lays, cols, dot(h, wd[:, cols]))

        tiles(8, 512, after)

    def backward(*ups):
        lays = [at.layer(up) for up in ups]
        rows = 128 * len(ups)
        low = {1: 0, 2: 256, 0: 384}[ups[0]]
        span = slice(low, low + rows)
        hg[0:rows] = jnp.zeros((rows, 192), F32)

        def before(j, cols):
            a = stacked(1, lays, cols, 1024)
            hg[0:rows] += lax.dot_general(a, wd[:, cols], NT, preferred_element_type=F32)

        tiles(4, 1024, before)
        g = pre_g[span]
        sig = jax.nn.sigmoid(g)
        grad = hg[0:rows] * scale[...]
        gate_delta = grad * pre_u[span] * sig * (1.0 + g * (1.0 - sig))
        up_delta = grad * (g * sig)
        gd = gate_delta.astype(BF)
        ud = up_delta.astype(BF)
        keep_t(del_t, 0, lays, gate_delta)
        keep_t(del_t, 192, lays, up_delta)

        def after(j, cols):
            spread(1, lays, cols, dot(gd, wg[:, cols]) + dot(ud, wu[:, cols]))

        tiles(8, 512, after)

    def trade(kind, up):
        slots = pl.ds(at.slot(up, 1, 0) - at.y, 4)
        sent.append(
            push(pp.at[kind, slots], pb.at[kind, up], es.at[kind, up], er.at[kind, up], at.partner)
        )

    def traded(kind, up):
        landed(pb.at[kind, up], er.at[kind, up], at.partner)

    def combine(kind, up, i, extra):
        parts = [pp.at[kind, at.slot(up, 0, i)], pb.at[kind, up, at.group(i)]] + extra

        def add(j, cols):
            acc = parts[0][:, cols].astype(F32)
            for part in parts[1:]:
                acc = acc + part[:, cols].astype(F32)
            parts[1][:, cols] = acc.astype(BF)

        tiles(4, 1024, add)
        return parts[1]

    def up_send(kind, src, k):
        sent.append(push(src, xp.at[kind, k], tps.at[kind, k], tpr.at[kind, k], at.above))

    def down_send(kind, src, k):
        sent.append(push(src, xm.at[kind, k], tms.at[kind, k], tmr.at[kind, k], at.below))

    def from_below(kind, k):
        landed(xp.at[kind, k], tpr.at[kind, k], at.above)
        return xp.at[kind, k]

    def from_above(kind, k):
        landed(xm.at[kind, k], tmr.at[kind, k], at.below)
        return xm.at[kind, k]

    def send_plain(kind):
        for k in range(2):
            up_send(kind, combine(kind, 1, DOWN[k], []), k)
            down_send(kind, combine(kind, 3, UP[k], []), k)

    def send_across(kind):
        for k in range(2):
            up_send(kind, combine(kind, 2, UP[k], []), 2 + k)
            down_send(kind, combine(kind, 2, DOWN[k], []), 2 + k)

    def send_merged(kind):
        for k in range(2):
            up_send(kind, combine(kind, 1, UP[k], [from_below(kind, 2 + k)]), 4 + k)
            down_send(kind, combine(kind, 3, DOWN[k], [from_above(kind, 2 + k)]), 4 + k)

    def send_home(kind):
        for i in (DOWN[0], UP[0], DOWN[1], UP[1]):
            if i in UP:
                k = UP.index(i)
                extra = [from_above(kind, k), from_below(kind, 4 + k)]
            else:
                k = DOWN.index(i)
                extra = [from_below(kind, k), from_above(kind, 4 + k)]
            sums = combine(kind, 0, i, extra)
            for x in range(4):
                om[kind, i * 4 + x] = sums[4 * x : 4 * x + 4, :]
            for j in (1, 3, 2, 0):
                e = at.in_plane(i, j)
                src = om.at[kind, i * 4 + lax.rem(at.x + j, 4)]
                k = i * 4 + j
                if k:
                    sent.append(
                        push(src, rb.at[kind, at.e], s3.at[kind, k], r3.at[kind, k], (at.s, e))
                    )
                else:
                    pltpu.make_async_copy(src, rb.at[kind, at.e], loc.at[7 + kind]).start()

    def came_home(kind):
        for i, j in HOPS:
            e = at.in_plane(4 - i, 4 - j)
            if i or j:
                landed(rb.at[kind, e], r3.at[kind, i * 4 + j], at.partner)
            else:
                pltpu.make_async_copy(om.at[kind, at.x], rb.at[kind, e], loc.at[7 + kind]).wait()
        for e in range(16):
            ret[kind, 4 * e : 4 * e + 4, :] = rb[kind, e]

    for i in range(4):
        gather(0, i)
    from_beside(0, 0)
    gather(1, 0)
    gather(1, 1)
    from_beside(0, 1)
    gather(1, 2)
    gather(1, 3)
    from_partner(0, 0)
    for load in loads[1:]:
        load.wait()
    forward(0)
    trade(0, 0)
    from_beside(0, 2)
    from_beside(0, 3)
    from_partner(0, 3)
    from_partner(0, 1)
    forward(1, 3)
    trade(0, 1)
    trade(0, 3)
    from_across(0, 0)
    from_across(0, 1)
    from_beside(1, 0)
    from_beside(1, 1)
    traded(0, 1)
    traded(0, 3)
    send_plain(0)
    from_partner(1, 0)
    backward(0)
    trade(1, 0)
    from_beside(1, 2)
    from_beside(1, 3)
    from_across(0, 2)
    from_across(0, 3)
    from_partner(0, 2)
    forward(2)
    trade(0, 2)
    from_across(1, 0)
    from_across(1, 1)
    traded(0, 2)
    send_across(0)
    from_partner(1, 3)
    from_partner(1, 1)
    backward(1, 3)
    trade(1, 1)
    trade(1, 3)
    from_across(1, 2)
    from_across(1, 3)
    traded(1, 1)
    traded(1, 3)
    send_plain(1)
    from_partner(1, 2)
    backward(2)
    trade(1, 2)
    send_merged(0)
    traded(1, 2)
    send_across(1)

    def weight_tile(j, cols):
        v = dot(del_t[...], xc[0, :, :, cols].reshape(512, 512))
        gate_w[:, cols] = v[0:192]
        up_w[:, cols] = v[192:384]
        c = xc[1, :, :, cols].reshape(512, 512)
        down_w[:, cols] = dot(hid_t[...], c)

    tiles(8, 512, weight_tile)
    traded(0, 0)
    send_home(0)
    send_merged(1)
    came_home(0)

    pulls = jnp.zeros((64, 1), F32)
    for j in range(4):
        cols = slice(1024 * j, 1024 * j + 1024)
        pulls = pulls + jnp.sum(
            pc[:, cols].astype(F32) * ret[0, :, cols].astype(F32), axis=1, keepdims=True
        )
    score = live * pulls * raw * (1.0 - raw)
    by_row = select * score
    sgt = lax.dot_general(mine16, by_row, TN, precision=HIGH, preferred_element_type=F32)
    sg = lax.dot_general(by_row, mine16, TN, precision=HIGH, preferred_element_type=F32)
    parts = joined(thirds(sgt), 0)
    bias = jnp.sum(sg, axis=0, keepdims=True)
    bias = jnp.concatenate([bias, jnp.zeros((1, 112), F32)], axis=1)
    bias = jnp.broadcast_to(bias, (16, 128))

    def router_tile(j, cols):
        v = dot(parts, tok[:, cols])
        core, lay = lax.rem(j, 2), lax.div(j, 2)
        t[core, lay, :, 0:512] = v[0:16] + v[16:32] + v[32:48]
        t[core, lay, :, 512:640] = bias

    tiles(8, 512, router_tile)
    sent.append(push(t.at[1 - at.c], ta, pas, par, at.partner))
    landed(ta, par, at.partner)
    tz[...] = t[at.c] + ta[...]
    for d in range(1, 4):
        sent.append(
            push(tz.at[at.layer(d)], tzr.at[d - 1], zs.at[d - 1], zr.at[d - 1], at.at_layer(d))
        )
    traded(1, 0)
    send_home(1)
    acc = tz[at.z]
    for d in range(3):
        landed(tzr.at[d], zr.at[d], at.partner)
        acc = acc + tzr[d]
    for y in range(4):
        ext[y, 0:16, :] = acc[:, 128 * y : 128 * y + 128]
        ext[y, 16:24, :] = acc[0:8, 512:640]
    for d, peer in enumerate(plane):
        sent.append(push(ext.at[lax.div(peer[1], 4)], tb.at[d], sb.at[d], rbs.at[d], peer))
    mix_w = joined(thirds((select * gate).T), 1)
    sg_w = joined(thirds(sg), 1)

    def mix_tile(j, cols):
        rows = ret[0, :, cols]
        mix[:, cols] = dot(mix_w, jnp.concatenate([rows] * 3, axis=0)).astype(BF)

    tiles(8, 512, mix_tile)
    def base_tile(j, cols):
        r = router[:, cols]
        base[:, cols] = dot(sg_w, jnp.concatenate([r] * 3, axis=0))

    tiles(8, 512, base_tile)
    for copy in sent:
        copy.wait_send()
    came_home(1)
    select_t = select.T.astype(BF)

    def grad_tile(j, cols):
        tgr[:, cols] = (base[:, cols] + dot(select_t, ret[1, :, cols])).astype(BF)

    tiles(8, 512, grad_tile)
    done = ext[at.y]
    for d in range(15):
        landed(tb.at[d], rbs.at[d], at.partner)
        done = done + tb[d]
    quarter = jnp.zeros((16, 32), F32)
    for x in range(4):
        quarter = jnp.where(at.x == x, done[0:16, 32 * x : 32 * x + 32], quarter)
    red[...] = quarter
    thr_out[...] = -done[16:17, 0:16]


def layer(tokens, cotangent, wg, wu, wd, router, thr, scale, picks, counts):
    vmem = pl.BlockSpec(memory_space=pltpu.VMEM)
    hbm = pl.BlockSpec(memory_space=pl.ANY)
    dma = pltpu.SemaphoreType.DMA
    v = pltpu.VMEM
    width = tokens.shape[1]
    units = wg.shape[0]
    return pl.pallas_call(
        layer_kernel,
        out_shape=(
            v((256, width), BF),
            v((256, width), BF),
            v((units, width), F32),
            v((units, width), F32),
            v((units, width), F32),
            v((16, 32), F32),
            v((1, 16), F32),
        ),
        in_specs=[hbm] * 5 + [vmem] * 5,
        out_specs=(vmem,) * 7,
        scratch_shapes=[
            v((256, width), BF), v((256, width), BF),
            v((units, width), BF), v((units, width), BF), v((units, width), BF),
            v((64, width), BF), v((64, width), BF), v((64, width), BF),
            v((2, 16, 4, width), BF), v((2, 16, 4, width), BF),
            v((2, 32, 16, width), BF), v((2, 32, 16, width), BF),
            v((2, 4, 4, 16, width), BF),
            v((2, 6, 16, width), BF), v((2, 6, 16, width), BF),
            v((2, 16, 4, width), BF), v((2, 16, 4, width), BF), v((2, 64, width), BF),
            v((512, units), F32), v((512, units), F32), v((256, units), F32),
            v((units, 512), BF), v((2 * units, 512), BF),
            v((256, width), F32),
            v((2, 4, 16, 640), F32), v((4, 16, 640), F32), v((4, 16, 640), F32),
            v((3, 16, 640), F32), v((4, 24, 128), F32), v((15, 24, 128), F32),
            dma((2, 16)), dma((2, 16)), dma((2, 6)), dma((2, 6)), dma((2, 6)), dma((2, 6)),
            dma((2, 16)), dma((2, 16)), dma((2, 4)), dma((2, 4)),
            dma((2, 6)), dma((2, 6)), dma((2, 6)), dma((2, 6)),
            dma((2, 16)), dma((2, 16)), dma, dma, dma((3,)), dma((3,)),
            dma((15,)), dma((15,)), dma((13,)),
        ],
        compiler_params=pltpu.CompilerParams(
            collective_id=0, has_side_effects=True, vmem_limit_bytes=49 << 20
        ),
    )(tokens, cotangent, wg, wu, wd, router, thr, scale, picks, counts)


def store_kernel(*refs):
    half = len(refs) // 2
    sems = refs[-1]
    copies = [
        pltpu.make_async_copy(refs[k], refs[half + k], sems.at[k]) for k in range(half)
    ]
    for copy in copies:
        copy.start()
    for copy in copies:
        copy.wait()


def store(values):
    held = [pltpu.with_memory_space_constraint(a, pltpu.VMEM) for a in values]
    return pl.pallas_call(
        store_kernel,
        out_shape=tuple(jax.ShapeDtypeStruct(a.shape, a.dtype) for a in values),
        in_specs=[pl.BlockSpec(memory_space=pltpu.VMEM)] * len(values),
        out_specs=tuple(pl.BlockSpec(memory_space=pl.ANY) for _ in values),
        scratch_shapes=[pltpu.SemaphoreType.DMA((len(values),))],
        compiler_params=pltpu.CompilerParams(vmem_limit_bytes=8 << 20),
    )(*held)


def on_device(tokens, cotangent, router, threshold, w_gate, w_up, w_down, hid_scale, picks, counts):
    results = layer(
        tokens, cotangent, w_gate[0].T, w_up[0].T, w_down[0], router.T,
        threshold[None, :], hid_scale, picks[0].T, counts,
    )
    mixture, token_grad, gate_grad, up_grad, down_grad, reduced, thresholds = store(results)
    return (
        mixture,
        token_grad,
        reduced.T,
        thresholds[0],
        gate_grad.T[None],
        up_grad.T[None],
        down_grad[None],
    )


def solution(mesh):
    placed = (
        P(("seq", "exp"), None),
        P(("seq", "exp"), None),
        P(),
        P(),
        P("exp", None, "seq"),
        P("exp", None, "seq"),
        P("exp", "seq", None),
        P("exp", "seq"),
        P(("seq", "exp"), None, None),
        P(("seq", "exp"), None),
    )
    return jax.shard_map(
        on_device,
        mesh=mesh,
        in_specs=placed,
        out_specs=(
            P(("seq", "exp"), None),
            P(("seq", "exp"), None),
            P(("seq", "exp"), None),
            P(),
            P("exp", None, "seq"),
            P("exp", None, "seq"),
            P("exp", "seq", None),
        ),
        check_vma=False,
    )
```

```python
import jax
import jax.numpy as jnp
from jax import lax
from jax.experimental import pallas as pl
from jax.experimental.pallas import tpu as pltpu
from jax.sharding import PartitionSpec as P

MESH = pl.DeviceIdType.MESH
BF = jnp.bfloat16
F32 = jnp.float32
HIGH = lax.Precision.HIGHEST
UP = (2, 0)
DOWN = (1, 3)


class Spot:
    def __init__(self):
        self.s = lax.axis_index("seq")
        self.e = lax.axis_index("exp")
        self.z = lax.div(self.s, 2)
        self.c = lax.rem(self.s, 2)
        self.y = lax.div(self.e, 4)
        self.x = lax.rem(self.e, 4)
        self.partner = (self.s + 1 - 2 * self.c, self.e)
        self.above = (self.layer(1) * 2 + self.c, self.e)
        self.below = (self.layer(3) * 2 + self.c, self.e)

    def layer(self, up):
        return lax.rem(self.z + up, 4)

    def group(self, i):
        return lax.rem(self.y + i, 4)

    def slot(self, up, other, i):
        core = self.c + other * (1 - 2 * self.c)
        return (self.layer(up) * 2 + core) * 4 + self.group(i)

    def in_plane(self, i, j):
        return lax.rem(self.y + i, 4) * 4 + lax.rem(self.x + j, 4)

    def at_layer(self, up):
        return (self.layer(up) * 2 + self.c, self.e)

    def plane_peers(self):
        return [(self.s, lax.rem(self.e + d, 16)) for d in range(1, 16)]

    def column_peers(self):
        return [(lax.rem(self.s + d, 8), self.e) for d in range(1, 8)]


def greet(peers):
    for peer in peers:
        pl.semaphore_signal(
            pltpu.get_barrier_semaphore(), inc=1, device_id=peer, device_id_type=MESH
        )


def greeted(count):
    pl.semaphore_wait(pltpu.get_barrier_semaphore(), count)


def push(src, dst, send_sem, recv_sem, device):
    copy = pltpu.make_async_remote_copy(
        src_ref=src,
        dst_ref=dst,
        send_sem=send_sem,
        recv_sem=recv_sem,
        device_id=device,
        device_id_type=MESH,
    )
    copy.start()
    return copy


def landed(dst, recv_sem, device):
    pltpu.make_async_remote_copy(
        src_ref=dst,
        dst_ref=dst,
        send_sem=recv_sem,
        recv_sem=recv_sem,
        device_id=device,
        device_id_type=MESH,
    ).wait_recv()


HOPS = [(i, j) for i in range(4) for j in (0, 1, 3, 2)]
NT = (((1,), (1,)), ((), ()))
TN = (((0,), (0,)), ((), ()))


def dot(a, b):
    return jnp.dot(a, b, preferred_element_type=F32)


def thirds(v):
    first = v.astype(BF)
    rest = v - first.astype(F32)
    second = rest.astype(BF)
    return first, second, (rest - second.astype(F32)).astype(BF)


def tiles(count, width, body):
    def step(j, carry):
        body(j, pl.ds(pl.multiple_of(j * width, width), width))
        return carry

    lax.fori_loop(0, count, step, 0)


def left(ref, send_sem, device):
    pltpu.make_async_remote_copy(
        src_ref=ref,
        dst_ref=ref,
        send_sem=send_sem,
        recv_sem=send_sem,
        device_id=device,
        device_id_type=MESH,
    ).wait_send()


def joined(pieces, axis):
    return jnp.concatenate([v.astype(F32) for v in pieces], axis=axis).astype(BF)


def layer_kernel(
    tok_h, cot_h, wg_h, wu_h, wd_h, router, thr, scale, picks, counts,
    mix, tgr, gate_w, up_w, down_w, red, thr_out,
    tok, cot, wg, wu, wd, xr, cr, pc, msg, buf, xc, pp, pb, xp, xm, om, rb, ret,
    pre_g, pre_u, hg, hid_t, del_t, base, t, ta, tz, tzr, ext, tb,
    s1, r1, sp, rp, sm, rm, sq, rq, es, er, tps, tpr, tms, tmr, s3, r3,
    pas, par, zs, zr, sb, rbs, loc,
):
    at = Spot()
    plane = at.plane_peers()
    column = at.column_peers()
    greet(plane + column)
    loads = [
        pltpu.make_async_copy(a, b, loc.at[k])
        for k, (a, b) in enumerate([(cot_h, cot), (wg_h, wg), (wu_h, wu), (wd_h, wd)])
    ]
    pieces = []
    for k in range(4):
        cols = slice(1024 * k, 1024 * k + 1024)
        pieces.append(pltpu.make_async_copy(tok_h.at[:, cols], tok.at[:, cols], loc.at[9 + k]))
        pieces[k].start()

    row = lax.broadcasted_iota(jnp.int32, (64, 16), 0)
    lane = lax.broadcasted_iota(jnp.int32, (64, 16), 1)
    mine16 = (lax.div(row, 4) == lane).astype(F32)
    turn = lax.rem(row, 4)
    listed = picks[...].astype(F32)
    wide = jnp.zeros((64, 16), F32)
    for k in range(4):
        wide = jnp.where(turn == k, listed[k : k + 1, :], wide)
    pick = jnp.sum(wide * mine16, axis=1, keepdims=True)
    limit = jnp.sum(mine16 * counts[...].astype(F32), axis=1, keepdims=True)
    live = (turn[:, 0:1].astype(F32) < limit).astype(F32)
    select = (
        pick == lax.broadcasted_iota(jnp.int32, (64, 256), 1).astype(F32)
    ).astype(F32)
    select_bf = select.astype(BF)
    loads[0].start()

    for k in range(4):
        cols = slice(1024 * k, 1024 * k + 1024)
        pieces[k].wait()
        xr[:, cols] = dot(select_bf, tok[:, cols]).astype(BF)
    for e in range(16):
        msg[0, e] = xr[4 * e : 4 * e + 4, :]
    greeted(22)

    sent = []

    def scatter(kind):
        mine = pltpu.make_async_copy(msg.at[kind, at.e], buf.at[kind, at.e], loc.at[5 + kind])
        mine.start()
        for i, j in HOPS:
            if i or j:
                e = at.in_plane(4 - i, j)
                sent.append(
                    push(
                        msg.at[kind, e], buf.at[kind, at.e], s1.at[kind], r1.at[kind, i],
                        (at.s, e),
                    )
                )
        mine.wait()

    scatter(0)
    gates = jax.nn.sigmoid(
        lax.dot_general(tok[...], router[...], NT, preferred_element_type=F32) - thr[...]
    )
    chosen_gates = jnp.dot(select, gates, precision=HIGH, preferred_element_type=F32)
    raw = jnp.sum(chosen_gates * mine16, axis=1, keepdims=True)
    gate = raw * live
    loads[0].wait()
    for load in loads[1:]:
        load.start()

    def take_cots(j, cols):
        cots = dot(select_bf, cot[:, cols])
        pc[:, cols] = cots.astype(BF)
        cr[:, cols] = (cots * gate).astype(BF)

    tiles(8, 512, take_cots)
    for e in range(16):
        msg[1, e] = cr[4 * e : 4 * e + 4, :]
    scatter(1)

    def hand_over(kind, slot, q):
        ref = xc.at[kind, slot]
        push(ref, ref, sq.at[kind], rq.at[kind, q // 4], at.partner)

    def climb(kind, slot, k):
        ref = xc.at[kind, slot]
        push(ref, ref, sp.at[kind], rp.at[kind, k], at.above)

    def sink(kind, slot, k):
        ref = xc.at[kind, slot]
        push(ref, ref, sm.at[kind], rm.at[kind, k], at.below)

    def gather(kind, i):
        group = at.group(i)
        slot = at.slot(0, 0, i)
        came = pl.ds(group * 4, 4 if i else 3)
        landed(buf.at[kind, came], r1.at[kind, i], at.partner)
        for x in range(4):
            xc[kind, slot, 4 * x : 4 * x + 4, :] = buf[kind, group * 4 + x]
        climb(kind, slot, i)
        sink(kind, slot, i)
        hand_over(kind, slot, i)

    def from_beside(kind, i):
        slot = at.slot(3, 0, i)
        landed(xc.at[kind, slot], rp.at[kind, i], at.above)
        if i in UP:
            climb(kind, slot, 4 + UP.index(i))
        hand_over(kind, slot, 4 + i)
        slot = at.slot(1, 0, i)
        landed(xc.at[kind, slot], rm.at[kind, i], at.below)
        if i in DOWN:
            sink(kind, slot, 4 + DOWN.index(i))
        hand_over(kind, slot, 8 + i)

    def from_across(kind, i):
        slot = at.slot(2, 0, i)
        if i in UP:
            landed(xc.at[kind, slot], rp.at[kind, 4 + UP.index(i)], at.above)
        else:
            landed(xc.at[kind, slot], rm.at[kind, 4 + DOWN.index(i)], at.below)
        hand_over(kind, slot, 12 + i)

    def from_partner(kind, up):
        slots = pl.ds(at.slot(up, 1, 0) - at.y, 4)
        landed(xc.at[kind, slots], rq.at[kind, (0, 2, 3, 1)[up]], at.partner)

    def stacked(kind, lays, cols, width):
        parts = [xc[kind, pl.ds(lay * 8, 8), :, cols].reshape(128, width) for lay in lays]
        return parts[0] if len(parts) == 1 else jnp.concatenate(parts, axis=0)

    def spread(kind, lays, cols, v):
        for n, lay in enumerate(lays):
            piece = v[128 * n : 128 * n + 128]
            pp[kind, pl.ds(lay * 8, 8), :, cols] = piece.astype(BF).reshape(8, 16, 512)

    def keep_t(ref, first, lays, v):
        for n, lay in enumerate(lays):
            cols = pl.ds(pl.multiple_of(lay * 128, 128), 128)
            ref[first : first + 192, cols] = v[128 * n : 128 * n + 128].T.astype(BF)

    def forward(*ups):
        lays = [at.layer(up) for up in ups]
        rows = 128 * len(ups)
        low = {1: 0, 2: 256, 0: 384}[ups[0]]
        span = slice(low, low + rows)
        pre_g[span] = jnp.zeros((rows, 192), F32)
        pre_u[span] = jnp.zeros((rows, 192), F32)

        def before(j, cols):
            a = stacked(0, lays, cols, 1024)
            pre_g[span] += lax.dot_general(a, wg[:, cols], NT, preferred_element_type=F32)
            pre_u[span] += lax.dot_general(a, wu[:, cols], NT, preferred_element_type=F32)

        tiles(4, 1024, before)
        g = pre_g[span]
        hidden = g * jax.nn.sigmoid(g) * pre_u[span] * scale[...]
        h = hidden.astype(BF)
        keep_t(hid_t, 0, lays, hidden)

        def after(j, cols):
            spread(0, lays, cols, dot(h, wd[:, cols]))

        tiles(8, 512, after)

    def backward(*ups):
        lays = [at.layer(up) for up in ups]
        rows = 128 * len(ups)
        low = {1: 0, 2: 256, 0: 384}[ups[0]]
        span = slice(low, low + rows)
        hg[0:rows] = jnp.zeros((rows, 192), F32)

        def before(j, cols):
            a = stacked(1, lays, cols, 1024)
            hg[0:rows] += lax.dot_general(a, wd[:, cols], NT, preferred_element_type=F32)

        tiles(4, 1024, before)
        g = pre_g[span]
        sig = jax.nn.sigmoid(g)
        grad = hg[0:rows] * scale[...]
        gate_delta = grad * pre_u[span] * sig * (1.0 + g * (1.0 - sig))
        up_delta = grad * (g * sig)
        gd = gate_delta.astype(BF)
        ud = up_delta.astype(BF)
        keep_t(del_t, 0, lays, gate_delta)
        keep_t(del_t, 192, lays, up_delta)

        def after(j, cols):
            spread(1, lays, cols, dot(gd, wg[:, cols]) + dot(ud, wu[:, cols]))

        tiles(8, 512, after)

    def trade(kind, up):
        slots = pl.ds(at.slot(up, 1, 0) - at.y, 4)
        sent.append(
            push(pp.at[kind, slots], pb.at[kind, up], es.at[kind], er.at[kind, up], at.partner)
        )

    def traded(kind, up):
        landed(pb.at[kind, up], er.at[kind, up], at.partner)

    def combine(kind, up, i, extra):
        parts = [pp.at[kind, at.slot(up, 0, i)], pb.at[kind, up, at.group(i)]] + extra

        def add(j, cols):
            acc = parts[0][:, cols].astype(F32)
            for part in parts[1:]:
                acc = acc + part[:, cols].astype(F32)
            parts[1][:, cols] = acc.astype(BF)

        tiles(4, 1024, add)
        return parts[1]

    def up_send(kind, src, k):
        push(src, xp.at[kind, k], tps.at[kind], tpr.at[kind, k], at.above)

    def down_send(kind, src, k):
        push(src, xm.at[kind, k], tms.at[kind], tmr.at[kind, k], at.below)

    def from_below(kind, k):
        landed(xp.at[kind, k], tpr.at[kind, k], at.above)
        return xp.at[kind, k]

    def from_above(kind, k):
        landed(xm.at[kind, k], tmr.at[kind, k], at.below)
        return xm.at[kind, k]

    def send_plain(kind):
        for k in range(2):
            up_send(kind, combine(kind, 1, DOWN[k], []), k)
            down_send(kind, combine(kind, 3, UP[k], []), k)

    def send_across(kind):
        for k in range(2):
            up_send(kind, combine(kind, 2, UP[k], []), 2 + k)
            down_send(kind, combine(kind, 2, DOWN[k], []), 2 + k)

    def send_merged(kind):
        for k in range(2):
            up_send(kind, combine(kind, 1, UP[k], [from_below(kind, 2 + k)]), 4 + k)
            down_send(kind, combine(kind, 3, DOWN[k], [from_above(kind, 2 + k)]), 4 + k)

    def send_home(kind):
        for i in (DOWN[0], UP[0], DOWN[1], UP[1]):
            if i in UP:
                k = UP.index(i)
                extra = [from_above(kind, k), from_below(kind, 4 + k)]
            else:
                k = DOWN.index(i)
                extra = [from_below(kind, k), from_above(kind, 4 + k)]
            sums = combine(kind, 0, i, extra)
            for x in range(4):
                om[kind, i * 4 + x] = sums[4 * x : 4 * x + 4, :]
            for j in (1, 3, 2, 0):
                e = at.in_plane(i, j)
                src = om.at[kind, i * 4 + lax.rem(at.x + j, 4)]
                if i or j:
                    sent.append(
                        push(src, rb.at[kind, at.e], s3.at[kind], r3.at[kind], (at.s, e))
                    )
                else:
                    pltpu.make_async_copy(src, rb.at[kind, at.e], loc.at[7 + kind]).start()

    def came_home(kind):
        pltpu.make_async_copy(om.at[kind, at.x], rb.at[kind, at.e], loc.at[7 + kind]).wait()
        landed(rb.at[kind, 0:15], r3.at[kind], at.partner)
        for e in range(16):
            ret[kind, 4 * e : 4 * e + 4, :] = rb[kind, e]

    for i in range(4):
        gather(0, i)
    from_beside(0, 0)
    gather(1, 0)
    gather(1, 1)
    from_beside(0, 1)
    gather(1, 2)
    gather(1, 3)
    from_partner(0, 0)
    for load in loads[1:]:
        load.wait()
    forward(0)
    trade(0, 0)
    from_beside(0, 2)
    from_beside(0, 3)
    from_partner(0, 3)
    from_partner(0, 1)
    forward(1, 3)
    trade(0, 1)
    trade(0, 3)
    from_across(0, 0)
    from_across(0, 1)
    from_beside(1, 0)
    from_beside(1, 1)
    traded(0, 1)
    traded(0, 3)
    send_plain(0)
    from_partner(1, 0)
    backward(0)
    trade(1, 0)
    from_beside(1, 2)
    from_beside(1, 3)
    from_across(0, 2)
    from_across(0, 3)
    from_partner(0, 2)
    forward(2)
    trade(0, 2)
    from_across(1, 0)
    from_across(1, 1)
    traded(0, 2)
    send_across(0)
    from_partner(1, 3)
    from_partner(1, 1)
    backward(1, 3)
    trade(1, 1)
    trade(1, 3)
    from_across(1, 2)
    from_across(1, 3)
    traded(1, 1)
    traded(1, 3)
    send_plain(1)
    from_partner(1, 2)
    backward(2)
    trade(1, 2)
    send_merged(0)
    traded(1, 2)
    send_across(1)

    def weight_tile(j, cols):
        v = dot(del_t[...], xc[0, :, :, cols].reshape(512, 512))
        gate_w[:, cols] = v[0:192]
        up_w[:, cols] = v[192:384]
        c = xc[1, :, :, cols].reshape(512, 512)
        down_w[:, cols] = dot(hid_t[...], c)

    tiles(8, 512, weight_tile)
    traded(0, 0)
    send_home(0)
    send_merged(1)
    came_home(0)

    pulls = jnp.zeros((64, 1), F32)
    for j in range(4):
        cols = slice(1024 * j, 1024 * j + 1024)
        pulls = pulls + jnp.sum(
            pc[:, cols].astype(F32) * ret[0, :, cols].astype(F32), axis=1, keepdims=True
        )
    score = live * pulls * raw * (1.0 - raw)
    by_row = select * score
    sgt = lax.dot_general(mine16, by_row, TN, precision=HIGH, preferred_element_type=F32)
    sg = lax.dot_general(by_row, mine16, TN, precision=HIGH, preferred_element_type=F32)
    parts = joined(thirds(sgt), 0)
    bias = jnp.sum(sg, axis=0, keepdims=True)
    bias = jnp.concatenate([bias, jnp.zeros((1, 112), F32)], axis=1)
    bias = jnp.broadcast_to(bias, (16, 128))

    def router_tile(j, cols):
        v = dot(parts, tok[:, cols])
        core, lay = lax.rem(j, 2), lax.div(j, 2)
        t[core, lay, :, 0:512] = v[0:16] + v[16:32] + v[32:48]
        t[core, lay, :, 512:640] = bias

    tiles(8, 512, router_tile)
    push(t.at[1 - at.c], ta, pas, par, at.partner)
    landed(ta, par, at.partner)
    tz[...] = t[at.c] + ta[...]
    for d in range(1, 4):
        sent.append(
            push(tz.at[at.layer(d)], tzr.at[d - 1], zs, zr, at.at_layer(d))
        )
    traded(1, 0)
    send_home(1)
    acc = tz[at.z]
    landed(tzr, zr, at.partner)
    for d in range(3):
        acc = acc + tzr[d]
    for y in range(4):
        ext[y, 0:16, :] = acc[:, 128 * y : 128 * y + 128]
        ext[y, 16:24, :] = acc[0:8, 512:640]
    for d, peer in enumerate(plane):
        push(ext.at[lax.div(peer[1], 4)], tb.at[d], sb, rbs, peer)
    mix_w = joined(thirds((select * gate).T), 1)
    sg_w = joined(thirds(sg), 1)

    def mix_tile(j, cols):
        rows = ret[0, :, cols]
        mix[:, cols] = dot(mix_w, jnp.concatenate([rows] * 3, axis=0)).astype(BF)

    tiles(8, 512, mix_tile)
    def base_tile(j, cols):
        r = router[:, cols]
        base[:, cols] = dot(sg_w, jnp.concatenate([r] * 3, axis=0))

    tiles(8, 512, base_tile)
    for kind in range(2):
        left(msg.at[kind, 0:15], s1.at[kind], at.partner)
        left(xc.at[kind, 0:6], sp.at[kind], at.partner)
        left(xc.at[kind, 0:6], sm.at[kind], at.partner)
        left(xc.at[kind, 0:16], sq.at[kind], at.partner)
        left(pb.at[kind], es.at[kind], at.partner)
        left(xp.at[kind], tps.at[kind], at.partner)
        left(xm.at[kind], tms.at[kind], at.partner)
        left(om.at[kind, 0:15], s3.at[kind], at.partner)
    left(ta, pas, at.partner)
    left(tzr, zs, at.partner)
    left(tb, sb, at.partner)
    came_home(1)
    select_t = select.T.astype(BF)

    def grad_tile(j, cols):
        tgr[:, cols] = (base[:, cols] + dot(select_t, ret[1, :, cols])).astype(BF)

    tiles(8, 512, grad_tile)
    done = ext[at.y]
    landed(tb, rbs, at.partner)
    for d in range(15):
        done = done + tb[d]
    quarter = jnp.zeros((16, 32), F32)
    for x in range(4):
        quarter = jnp.where(at.x == x, done[0:16, 32 * x : 32 * x + 32], quarter)
    red[...] = quarter
    thr_out[...] = -done[16:17, 0:16]


def layer(tokens, cotangent, wg, wu, wd, router, thr, scale, picks, counts):
    vmem = pl.BlockSpec(memory_space=pltpu.VMEM)
    hbm = pl.BlockSpec(memory_space=pl.ANY)
    dma = pltpu.SemaphoreType.DMA
    v = pltpu.VMEM
    width = tokens.shape[1]
    units = wg.shape[0]
    return pl.pallas_call(
        layer_kernel,
        out_shape=(
            v((256, width), BF),
            v((256, width), BF),
            v((units, width), F32),
            v((units, width), F32),
            v((units, width), F32),
            v((16, 32), F32),
            v((1, 16), F32),
        ),
        in_specs=[hbm] * 5 + [vmem] * 5,
        out_specs=(vmem,) * 7,
        scratch_shapes=[
            v((256, width), BF), v((256, width), BF),
            v((units, width), BF), v((units, width), BF), v((units, width), BF),
            v((64, width), BF), v((64, width), BF), v((64, width), BF),
            v((2, 16, 4, width), BF), v((2, 16, 4, width), BF),
            v((2, 32, 16, width), BF), v((2, 32, 16, width), BF),
            v((2, 4, 4, 16, width), BF),
            v((2, 6, 16, width), BF), v((2, 6, 16, width), BF),
            v((2, 16, 4, width), BF), v((2, 16, 4, width), BF), v((2, 64, width), BF),
            v((512, units), F32), v((512, units), F32), v((256, units), F32),
            v((units, 512), BF), v((2 * units, 512), BF),
            v((256, width), F32),
            v((2, 4, 16, 640), F32), v((4, 16, 640), F32), v((4, 16, 640), F32),
            v((3, 16, 640), F32), v((4, 24, 128), F32), v((15, 24, 128), F32),
            dma((2,)), dma((2, 4)), dma((2,)), dma((2, 6)), dma((2,)), dma((2, 6)),
            dma((2,)), dma((2, 4)), dma((2,)), dma((2, 4)),
            dma((2,)), dma((2, 6)), dma((2,)), dma((2, 6)),
            dma((2,)), dma((2,)), dma, dma, dma, dma, dma, dma, dma((13,)),
        ],
        compiler_params=pltpu.CompilerParams(
            collective_id=0, has_side_effects=True, vmem_limit_bytes=49 << 20
        ),
    )(tokens, cotangent, wg, wu, wd, router, thr, scale, picks, counts)


def store_kernel(*refs):
    half = len(refs) // 2
    sems = refs[-1]
    copies = [
        pltpu.make_async_copy(refs[k], refs[half + k], sems.at[k]) for k in range(half)
    ]
    for copy in copies:
        copy.start()
    for copy in copies:
        copy.wait()


def store(values):
    held = [pltpu.with_memory_space_constraint(a, pltpu.VMEM) for a in values]
    return pl.pallas_call(
        store_kernel,
        out_shape=tuple(jax.ShapeDtypeStruct(a.shape, a.dtype) for a in values),
        in_specs=[pl.BlockSpec(memory_space=pltpu.VMEM)] * len(values),
        out_specs=tuple(pl.BlockSpec(memory_space=pl.ANY) for _ in values),
        scratch_shapes=[pltpu.SemaphoreType.DMA((len(values),))],
        compiler_params=pltpu.CompilerParams(vmem_limit_bytes=8 << 20),
    )(*held)


def on_device(tokens, cotangent, router, threshold, w_gate, w_up, w_down, hid_scale, picks, counts):
    results = layer(
        tokens, cotangent, w_gate[0].T, w_up[0].T, w_down[0], router.T,
        threshold[None, :], hid_scale, picks[0].T, counts,
    )
    mixture, token_grad, gate_grad, up_grad, down_grad, reduced, thresholds = store(results)
    return (
        mixture,
        token_grad,
        reduced.T,
        thresholds[0],
        gate_grad.T[None],
        up_grad.T[None],
        down_grad[None],
    )


def solution(mesh):
    placed = (
        P(("seq", "exp"), None),
        P(("seq", "exp"), None),
        P(),
        P(),
        P("exp", None, "seq"),
        P("exp", None, "seq"),
        P("exp", "seq", None),
        P("exp", "seq"),
        P(("seq", "exp"), None, None),
        P(("seq", "exp"), None),
    )
    return jax.shard_map(
        on_device,
        mesh=mesh,
        in_specs=placed,
        out_specs=(
            P(("seq", "exp"), None),
            P(("seq", "exp"), None),
            P(("seq", "exp"), None),
            P(),
            P("exp", None, "seq"),
            P("exp", None, "seq"),
            P("exp", "seq", None),
        ),
        check_vma=False,
    )
```

```python
import jax
import jax.numpy as jnp
from jax import lax
from jax.experimental import pallas as pl
from jax.experimental.pallas import tpu as pltpu
from jax.sharding import PartitionSpec as P

MESH = pl.DeviceIdType.MESH
BF = jnp.bfloat16
F32 = jnp.float32
HIGH = lax.Precision.HIGHEST
UP = (2, 0)
DOWN = (1, 3)


class Spot:
    def __init__(self):
        self.s = lax.axis_index("seq")
        self.e = lax.axis_index("exp")
        self.z = lax.div(self.s, 2)
        self.c = lax.rem(self.s, 2)
        self.y = lax.div(self.e, 4)
        self.x = lax.rem(self.e, 4)
        self.partner = (self.s + 1 - 2 * self.c, self.e)
        self.above = (self.layer(1) * 2 + self.c, self.e)
        self.below = (self.layer(3) * 2 + self.c, self.e)

    def layer(self, up):
        return lax.rem(self.z + up, 4)

    def group(self, i):
        return lax.rem(self.y + i, 4)

    def slot(self, up, other, i):
        core = self.c + other * (1 - 2 * self.c)
        return (self.layer(up) * 2 + core) * 4 + self.group(i)

    def in_plane(self, i, j):
        return lax.rem(self.y + i, 4) * 4 + lax.rem(self.x + j, 4)

    def at_layer(self, up):
        return (self.layer(up) * 2 + self.c, self.e)

    def plane_peers(self):
        return [(self.s, lax.rem(self.e + d, 16)) for d in range(1, 16)]

    def column_peers(self):
        return [(lax.rem(self.s + d, 8), self.e) for d in range(1, 8)]


def greet(peers):
    for peer in peers:
        pl.semaphore_signal(
            pltpu.get_barrier_semaphore(), inc=1, device_id=peer, device_id_type=MESH
        )


def greeted(count):
    pl.semaphore_wait(pltpu.get_barrier_semaphore(), count)


def push(src, dst, send_sem, recv_sem, device):
    copy = pltpu.make_async_remote_copy(
        src_ref=src,
        dst_ref=dst,
        send_sem=send_sem,
        recv_sem=recv_sem,
        device_id=device,
        device_id_type=MESH,
    )
    copy.start()
    return copy


def landed(dst, recv_sem, device):
    pltpu.make_async_remote_copy(
        src_ref=dst,
        dst_ref=dst,
        send_sem=recv_sem,
        recv_sem=recv_sem,
        device_id=device,
        device_id_type=MESH,
    ).wait_recv()


HOPS = [(i, j) for i in range(4) for j in (0, 2, 1, 3)]
NT = (((1,), (1,)), ((), ()))
TN = (((0,), (0,)), ((), ()))


def dot(a, b):
    return jnp.dot(a, b, preferred_element_type=F32)


def thirds(v):
    first = v.astype(BF)
    rest = v - first.astype(F32)
    second = rest.astype(BF)
    return first, second, (rest - second.astype(F32)).astype(BF)


def tiles(count, width, body):
    def step(j, carry):
        body(j, pl.ds(pl.multiple_of(j * width, width), width))
        return carry

    lax.fori_loop(0, count, step, 0)


def left(ref, send_sem, device):
    pltpu.make_async_remote_copy(
        src_ref=ref,
        dst_ref=ref,
        send_sem=send_sem,
        recv_sem=send_sem,
        device_id=device,
        device_id_type=MESH,
    ).wait_send()


def joined(pieces, axis):
    return jnp.concatenate([v.astype(F32) for v in pieces], axis=axis).astype(BF)


def layer_kernel(
    tok_h, cot_h, wg_h, wu_h, wd_h, router, thr, scale, picks, counts,
    mix, tgr, gate_w, up_w, down_w, red, thr_out,
    tok, cot, wg, wu, wd, xr, cr, pc, msg, buf, xc, pp, pb, xp, xm, om, rb, ret,
    pre_g, pre_u, hg, hid_t, del_t, base, t, ta, tz, tzr, ext, tb,
    s1, r1, sp, rp, sm, rm, sq, rq, es, er, tps, tpr, tms, tmr, s3, r3,
    pas, par, zs, zr, sb, rbs, loc,
):
    at = Spot()
    plane = at.plane_peers()
    column = at.column_peers()
    loads = [
        pltpu.make_async_copy(a, b, loc.at[k])
        for k, (a, b) in enumerate([(cot_h, cot), (wg_h, wg), (wu_h, wu), (wd_h, wd)])
    ]
    pieces = []
    for k in range(4):
        cols = slice(1024 * k, 1024 * k + 1024)
        pieces.append(pltpu.make_async_copy(tok_h.at[:, cols], tok.at[:, cols], loc.at[9 + k]))
        pieces[k].start()
    greet(plane + column)

    row = lax.broadcasted_iota(jnp.int32, (64, 16), 0)
    lane = lax.broadcasted_iota(jnp.int32, (64, 16), 1)
    mine16 = (lax.div(row, 4) == lane).astype(F32)
    turn = lax.rem(row, 4)
    listed = picks[...].astype(F32)
    wide = jnp.zeros((64, 16), F32)
    for k in range(4):
        wide = jnp.where(turn == k, listed[k : k + 1, :], wide)
    pick = jnp.sum(wide * mine16, axis=1, keepdims=True)
    limit = jnp.sum(mine16 * counts[...].astype(F32), axis=1, keepdims=True)
    live = (turn[:, 0:1].astype(F32) < limit).astype(F32)
    select = (
        pick == lax.broadcasted_iota(jnp.int32, (64, 256), 1).astype(F32)
    ).astype(F32)
    select_bf = select.astype(BF)
    loads[0].start()

    for k in range(4):
        cols = slice(1024 * k, 1024 * k + 1024)
        pieces[k].wait()
        xr[:, cols] = dot(select_bf, tok[:, cols]).astype(BF)
    for e in range(16):
        msg[0, e] = xr[4 * e : 4 * e + 4, :]
    greeted(22)

    sent = []

    def scatter(kind):
        mine = pltpu.make_async_copy(msg.at[kind, at.e], buf.at[kind, at.e], loc.at[5 + kind])
        mine.start()
        for i, j in HOPS:
            if i or j:
                e = at.in_plane(4 - i, j)
                sent.append(
                    push(
                        msg.at[kind, e], buf.at[kind, at.e], s1.at[kind], r1.at[kind, i],
                        (at.s, e),
                    )
                )
        mine.wait()

    scatter(0)
    gates = jax.nn.sigmoid(
        lax.dot_general(tok[...], router[...], NT, preferred_element_type=F32) - thr[...]
    )
    chosen_gates = jnp.dot(select, gates, precision=HIGH, preferred_element_type=F32)
    raw = jnp.sum(chosen_gates * mine16, axis=1, keepdims=True)
    gate = raw * live
    loads[0].wait()
    for load in loads[1:]:
        load.start()

    def take_cots(j, cols):
        cots = dot(select_bf, cot[:, cols])
        pc[:, cols] = cots.astype(BF)
        cr[:, cols] = (cots * gate).astype(BF)

    tiles(8, 512, take_cots)
    for e in range(16):
        msg[1, e] = cr[4 * e : 4 * e + 4, :]
    scatter(1)

    def hand_over(kind, slot, q):
        ref = xc.at[kind, slot]
        push(ref, ref, sq.at[kind], rq.at[kind, q // 4], at.partner)

    def climb(kind, slot, k):
        ref = xc.at[kind, slot]
        push(ref, ref, sp.at[kind], rp.at[kind, k], at.above)

    def sink(kind, slot, k):
        ref = xc.at[kind, slot]
        push(ref, ref, sm.at[kind], rm.at[kind, k], at.below)

    def gather(kind, i):
        group = at.group(i)
        slot = at.slot(0, 0, i)
        came = pl.ds(group * 4, 4 if i else 3)
        landed(buf.at[kind, came], r1.at[kind, i], at.partner)
        for x in range(4):
            xc[kind, slot, 4 * x : 4 * x + 4, :] = buf[kind, group * 4 + x]
        climb(kind, slot, i)
        sink(kind, slot, i)
        hand_over(kind, slot, i)

    def from_beside(kind, i):
        slot = at.slot(3, 0, i)
        landed(xc.at[kind, slot], rp.at[kind, i], at.above)
        if i in UP:
            climb(kind, slot, 4 + UP.index(i))
        hand_over(kind, slot, 4 + i)
        slot = at.slot(1, 0, i)
        landed(xc.at[kind, slot], rm.at[kind, i], at.below)
        if i in DOWN:
            sink(kind, slot, 4 + DOWN.index(i))
        hand_over(kind, slot, 8 + i)

    def from_across(kind, i):
        slot = at.slot(2, 0, i)
        if i in UP:
            landed(xc.at[kind, slot], rp.at[kind, 4 + UP.index(i)], at.above)
        else:
            landed(xc.at[kind, slot], rm.at[kind, 4 + DOWN.index(i)], at.below)
        hand_over(kind, slot, 12 + i)

    def from_partner(kind, up):
        slots = pl.ds(at.slot(up, 1, 0) - at.y, 4)
        landed(xc.at[kind, slots], rq.at[kind, (0, 2, 3, 1)[up]], at.partner)

    def stacked(kind, lays, cols, width):
        parts = [xc[kind, pl.ds(lay * 8, 8), :, cols].reshape(128, width) for lay in lays]
        return parts[0] if len(parts) == 1 else jnp.concatenate(parts, axis=0)

    def spread(kind, lays, cols, v):
        for n, lay in enumerate(lays):
            piece = v[128 * n : 128 * n + 128]
            pp[kind, pl.ds(lay * 8, 8), :, cols] = piece.astype(BF).reshape(8, 16, 512)

    def keep_t(ref, first, lays, v):
        for n, lay in enumerate(lays):
            cols = pl.ds(pl.multiple_of(lay * 128, 128), 128)
            ref[first : first + 192, cols] = v[128 * n : 128 * n + 128].T.astype(BF)

    def forward(*ups):
        lays = [at.layer(up) for up in ups]
        rows = 128 * len(ups)
        low = {1: 0, 2: 256, 0: 384}[ups[0]]
        span = slice(low, low + rows)
        pre_g[span] = jnp.zeros((rows, 192), F32)
        pre_u[span] = jnp.zeros((rows, 192), F32)

        def before(j, cols):
            a = stacked(0, lays, cols, 1024)
            pre_g[span] += lax.dot_general(a, wg[:, cols], NT, preferred_element_type=F32)
            pre_u[span] += lax.dot_general(a, wu[:, cols], NT, preferred_element_type=F32)

        tiles(4, 1024, before)
        g = pre_g[span]
        hidden = g * jax.nn.sigmoid(g) * pre_u[span] * scale[...]
        h = hidden.astype(BF)
        keep_t(hid_t, 0, lays, hidden)

        def after(j, cols):
            spread(0, lays, cols, dot(h, wd[:, cols]))

        tiles(8, 512, after)

    def backward(*ups):
        lays = [at.layer(up) for up in ups]
        rows = 128 * len(ups)
        low = {1: 0, 2: 256, 0: 384}[ups[0]]
        span = slice(low, low + rows)
        hg[0:rows] = jnp.zeros((rows, 192), F32)

        def before(j, cols):
            a = stacked(1, lays, cols, 1024)
            hg[0:rows] += lax.dot_general(a, wd[:, cols], NT, preferred_element_type=F32)

        tiles(4, 1024, before)
        g = pre_g[span]
        sig = jax.nn.sigmoid(g)
        grad = hg[0:rows] * scale[...]
        gate_delta = grad * pre_u[span] * sig * (1.0 + g * (1.0 - sig))
        up_delta = grad * (g * sig)
        gd = gate_delta.astype(BF)
        ud = up_delta.astype(BF)
        keep_t(del_t, 0, lays, gate_delta)
        keep_t(del_t, 192, lays, up_delta)

        def after(j, cols):
            spread(1, lays, cols, dot(gd, wg[:, cols]) + dot(ud, wu[:, cols]))

        tiles(8, 512, after)

    def trade(kind, up):
        slots = pl.ds(at.slot(up, 1, 0) - at.y, 4)
        sent.append(
            push(pp.at[kind, slots], pb.at[kind, up], es.at[kind], er.at[kind, up], at.partner)
        )

    def traded(kind, up):
        landed(pb.at[kind, up], er.at[kind, up], at.partner)

    def combine(kind, up, i, extra):
        parts = [pp.at[kind, at.slot(up, 0, i)], pb.at[kind, up, at.group(i)]] + extra

        def add(j, cols):
            acc = parts[0][:, cols].astype(F32)
            for part in parts[1:]:
                acc = acc + part[:, cols].astype(F32)
            parts[1][:, cols] = acc.astype(BF)

        tiles(4, 1024, add)
        return parts[1]

    def up_send(kind, src, k):
        push(src, xp.at[kind, k], tps.at[kind], tpr.at[kind, k], at.above)

    def down_send(kind, src, k):
        push(src, xm.at[kind, k], tms.at[kind], tmr.at[kind, k], at.below)

    def from_below(kind, k):
        landed(xp.at[kind, k], tpr.at[kind, k], at.above)
        return xp.at[kind, k]

    def from_above(kind, k):
        landed(xm.at[kind, k], tmr.at[kind, k], at.below)
        return xm.at[kind, k]

    def send_plain(kind):
        for k in range(2):
            up_send(kind, combine(kind, 1, DOWN[k], []), k)
            down_send(kind, combine(kind, 3, UP[k], []), k)

    def send_across(kind):
        for k in range(2):
            up_send(kind, combine(kind, 2, UP[k], []), 2 + k)
            down_send(kind, combine(kind, 2, DOWN[k], []), 2 + k)

    def send_merged(kind):
        for k in range(2):
            up_send(kind, combine(kind, 1, UP[k], [from_below(kind, 2 + k)]), 4 + k)
            down_send(kind, combine(kind, 3, DOWN[k], [from_above(kind, 2 + k)]), 4 + k)

    def send_home(kind):
        for i in (DOWN[0], UP[0], DOWN[1], UP[1]):
            if i in UP:
                k = UP.index(i)
                extra = [from_above(kind, k), from_below(kind, 4 + k)]
            else:
                k = DOWN.index(i)
                extra = [from_below(kind, k), from_above(kind, 4 + k)]
            sums = combine(kind, 0, i, extra)
            for x in range(4):
                om[kind, i * 4 + x] = sums[4 * x : 4 * x + 4, :]
            for j in (2, 1, 3, 0):
                e = at.in_plane(i, j)
                src = om.at[kind, i * 4 + lax.rem(at.x + j, 4)]
                if i or j:
                    sent.append(
                        push(src, rb.at[kind, at.e], s3.at[kind], r3.at[kind], (at.s, e))
                    )
                else:
                    pltpu.make_async_copy(src, rb.at[kind, at.e], loc.at[7 + kind]).start()

    def came_home(kind):
        pltpu.make_async_copy(om.at[kind, at.x], rb.at[kind, at.e], loc.at[7 + kind]).wait()
        landed(rb.at[kind, 0:15], r3.at[kind], at.partner)
        for e in range(16):
            ret[kind, 4 * e : 4 * e + 4, :] = rb[kind, e]

    for i in range(4):
        gather(0, i)
    from_beside(0, 0)
    gather(1, 0)
    gather(1, 1)
    from_beside(0, 1)
    gather(1, 2)
    gather(1, 3)
    from_partner(0, 0)
    for load in loads[1:]:
        load.wait()
    forward(0)
    trade(0, 0)
    from_beside(0, 2)
    from_beside(0, 3)
    from_partner(0, 3)
    from_partner(0, 1)
    forward(1, 3)
    trade(0, 1)
    trade(0, 3)
    from_across(0, 0)
    from_across(0, 1)
    from_beside(1, 0)
    from_beside(1, 1)
    traded(0, 1)
    traded(0, 3)
    send_plain(0)
    from_partner(1, 0)
    backward(0)
    trade(1, 0)
    from_beside(1, 2)
    from_beside(1, 3)
    from_across(0, 2)
    from_across(0, 3)
    from_partner(0, 2)
    forward(2)
    trade(0, 2)
    from_across(1, 0)
    from_across(1, 1)
    traded(0, 2)
    send_across(0)
    from_partner(1, 3)
    from_partner(1, 1)
    backward(1, 3)
    trade(1, 1)
    trade(1, 3)
    from_across(1, 2)
    from_across(1, 3)
    traded(1, 1)
    traded(1, 3)
    send_plain(1)
    from_partner(1, 2)
    backward(2)
    trade(1, 2)
    send_merged(0)
    traded(1, 2)
    send_across(1)

    def weight_tile(j, cols):
        v = dot(del_t[...], xc[0, :, :, cols].reshape(512, 512))
        gate_w[:, cols] = v[0:192]
        up_w[:, cols] = v[192:384]
        c = xc[1, :, :, cols].reshape(512, 512)
        down_w[:, cols] = dot(hid_t[...], c)

    tiles(8, 512, weight_tile)
    traded(0, 0)
    send_home(0)
    send_merged(1)
    came_home(0)

    pulls = jnp.zeros((64, 1), F32)
    for j in range(4):
        cols = slice(1024 * j, 1024 * j + 1024)
        pulls = pulls + jnp.sum(
            pc[:, cols].astype(F32) * ret[0, :, cols].astype(F32), axis=1, keepdims=True
        )
    score = live * pulls * raw * (1.0 - raw)
    by_row = select * score
    sgt = lax.dot_general(mine16, by_row, TN, precision=HIGH, preferred_element_type=F32)
    sg = lax.dot_general(by_row, mine16, TN, precision=HIGH, preferred_element_type=F32)
    parts = joined(thirds(sgt), 0)
    bias = jnp.sum(sg, axis=0, keepdims=True)
    bias = jnp.concatenate([bias, jnp.zeros((1, 112), F32)], axis=1)
    bias = jnp.broadcast_to(bias, (16, 128))

    def router_tile(j, cols):
        v = dot(parts, tok[:, cols])
        core, lay = lax.rem(j, 2), lax.div(j, 2)
        t[core, lay, :, 0:512] = v[0:16] + v[16:32] + v[32:48]
        t[core, lay, :, 512:640] = bias

    tiles(8, 512, router_tile)
    push(t.at[1 - at.c], ta, pas, par, at.partner)
    landed(ta, par, at.partner)
    tz[...] = t[at.c] + ta[...]
    for d in range(1, 4):
        sent.append(
            push(tz.at[at.layer(d)], tzr.at[d - 1], zs, zr, at.at_layer(d))
        )
    traded(1, 0)
    send_home(1)
    acc = tz[at.z]
    landed(tzr, zr, at.partner)
    for d in range(3):
        acc = acc + tzr[d]
    for y in range(4):
        ext[y, 0:16, :] = acc[:, 128 * y : 128 * y + 128]
        ext[y, 16:24, :] = acc[0:8, 512:640]
    for d, peer in enumerate(plane):
        push(ext.at[lax.div(peer[1], 4)], tb.at[d], sb, rbs, peer)
    mix_w = joined(thirds((select * gate).T), 1)
    sg_w = joined(thirds(sg), 1)

    def mix_tile(j, cols):
        rows = ret[0, :, cols]
        mix[:, cols] = dot(mix_w, jnp.concatenate([rows] * 3, axis=0)).astype(BF)

    tiles(8, 512, mix_tile)
    def base_tile(j, cols):
        r = router[:, cols]
        base[:, cols] = dot(sg_w, jnp.concatenate([r] * 3, axis=0))

    tiles(8, 512, base_tile)
    for kind in range(2):
        left(msg.at[kind, 0:15], s1.at[kind], at.partner)
        left(xc.at[kind, 0:6], sp.at[kind], at.partner)
        left(xc.at[kind, 0:6], sm.at[kind], at.partner)
        left(xc.at[kind, 0:16], sq.at[kind], at.partner)
        left(pb.at[kind], es.at[kind], at.partner)
        left(xp.at[kind], tps.at[kind], at.partner)
        left(xm.at[kind], tms.at[kind], at.partner)
        left(om.at[kind, 0:15], s3.at[kind], at.partner)
    left(ta, pas, at.partner)
    left(tzr, zs, at.partner)
    left(tb, sb, at.partner)
    came_home(1)
    select_t = select.T.astype(BF)

    def grad_tile(j, cols):
        tgr[:, cols] = (base[:, cols] + dot(select_t, ret[1, :, cols])).astype(BF)

    tiles(4, 1024, grad_tile)
    done = ext[at.y]
    landed(tb, rbs, at.partner)
    for d in range(15):
        done = done + tb[d]
    quarter = jnp.zeros((16, 32), F32)
    for x in range(4):
        quarter = jnp.where(at.x == x, done[0:16, 32 * x : 32 * x + 32], quarter)
    red[...] = quarter
    thr_out[...] = -done[16:17, 0:16]


def layer(tokens, cotangent, wg, wu, wd, router, thr, scale, picks, counts):
    vmem = pl.BlockSpec(memory_space=pltpu.VMEM)
    hbm = pl.BlockSpec(memory_space=pl.ANY)
    dma = pltpu.SemaphoreType.DMA
    v = pltpu.VMEM
    width = tokens.shape[1]
    units = wg.shape[0]
    return pl.pallas_call(
        layer_kernel,
        out_shape=(
            v((256, width), BF),
            v((256, width), BF),
            v((units, width), F32),
            v((units, width), F32),
            v((units, width), F32),
            v((16, 32), F32),
            v((1, 16), F32),
        ),
        in_specs=[hbm] * 5 + [vmem] * 5,
        out_specs=(vmem,) * 7,
        scratch_shapes=[
            v((256, width), BF), v((256, width), BF),
            v((units, width), BF), v((units, width), BF), v((units, width), BF),
            v((64, width), BF), v((64, width), BF), v((64, width), BF),
            v((2, 16, 4, width), BF), v((2, 16, 4, width), BF),
            v((2, 32, 16, width), BF), v((2, 32, 16, width), BF),
            v((2, 4, 4, 16, width), BF),
            v((2, 6, 16, width), BF), v((2, 6, 16, width), BF),
            v((2, 16, 4, width), BF), v((2, 16, 4, width), BF), v((2, 64, width), BF),
            v((512, units), F32), v((512, units), F32), v((256, units), F32),
            v((units, 512), BF), v((2 * units, 512), BF),
            v((256, width), F32),
            v((2, 4, 16, 640), F32), v((4, 16, 640), F32), v((4, 16, 640), F32),
            v((3, 16, 640), F32), v((4, 24, 128), F32), v((15, 24, 128), F32),
            dma((2,)), dma((2, 4)), dma((2,)), dma((2, 6)), dma((2,)), dma((2, 6)),
            dma((2,)), dma((2, 4)), dma((2,)), dma((2, 4)),
            dma((2,)), dma((2, 6)), dma((2,)), dma((2, 6)),
            dma((2,)), dma((2,)), dma, dma, dma, dma, dma, dma, dma((13,)),
        ],
        compiler_params=pltpu.CompilerParams(
            collective_id=0, has_side_effects=True, vmem_limit_bytes=49 << 20
        ),
    )(tokens, cotangent, wg, wu, wd, router, thr, scale, picks, counts)


def store_kernel(*refs):
    half = len(refs) // 2
    sems = refs[-1]
    copies = [
        pltpu.make_async_copy(refs[k], refs[half + k], sems.at[k]) for k in range(half)
    ]
    for copy in copies:
        copy.start()
    for copy in copies:
        copy.wait()


def store(values):
    held = [pltpu.with_memory_space_constraint(a, pltpu.VMEM) for a in values]
    return pl.pallas_call(
        store_kernel,
        out_shape=tuple(jax.ShapeDtypeStruct(a.shape, a.dtype) for a in values),
        in_specs=[pl.BlockSpec(memory_space=pltpu.VMEM)] * len(values),
        out_specs=tuple(pl.BlockSpec(memory_space=pl.ANY) for _ in values),
        scratch_shapes=[pltpu.SemaphoreType.DMA((len(values),))],
        compiler_params=pltpu.CompilerParams(vmem_limit_bytes=8 << 20),
    )(*held)


def on_device(tokens, cotangent, router, threshold, w_gate, w_up, w_down, hid_scale, picks, counts):
    results = layer(
        tokens, cotangent, w_gate[0].T, w_up[0].T, w_down[0], router.T,
        threshold[None, :], hid_scale, picks[0].T, counts,
    )
    mixture, token_grad, gate_grad, up_grad, down_grad, reduced, thresholds = store(results)
    return (
        mixture,
        token_grad,
        reduced.T,
        thresholds[0],
        gate_grad.T[None],
        up_grad.T[None],
        down_grad[None],
    )


def solution(mesh):
    placed = (
        P(("seq", "exp"), None),
        P(("seq", "exp"), None),
        P(),
        P(),
        P("exp", None, "seq"),
        P("exp", None, "seq"),
        P("exp", "seq", None),
        P("exp", "seq"),
        P(("seq", "exp"), None, None),
        P(("seq", "exp"), None),
    )
    return jax.shard_map(
        on_device,
        mesh=mesh,
        in_specs=placed,
        out_specs=(
            P(("seq", "exp"), None),
            P(("seq", "exp"), None),
            P(("seq", "exp"), None),
            P(),
            P("exp", None, "seq"),
            P("exp", None, "seq"),
            P("exp", "seq", None),
        ),
        check_vma=False,
    )
```
